32 devices in a mesh: groups: 2 (over y), seq: 4 (over z), head: 2 (over x), fsdp: 2 (over core).
Axes of the slice: x: 2, y: 2, z: 4, core: 2. Of those that a mesh axis runs over, the one named last changes fastest.
Arguments:
- residual_in: bfloat16 [16384, 2048], P(('groups', 'seq', 'fsdp'), 'head'), parts along dimension 0, may hold values from -6 to 6
- query_rows: bfloat16 [16384, 2048], P(('groups', 'seq', 'fsdp'), 'head'), parts along dimension 0, may hold values from -7 to 7
- key_rows: bfloat16 [16384, 2048], P(('groups', 'seq', 'fsdp'), 'head'), parts along dimension 0, may hold values from -7 to 7
- value_rows: bfloat16 [16384, 2048], P(('groups', 'seq', 'fsdp'), 'head'), parts along dimension 0, may hold values from -6 to 6
- bc_weight: bfloat16 [2048, 256], P(('head', 'fsdp')), may hold values from -0.125 to 0.125
- decay_rate: float32 [16384, 32], P(('groups', 'seq', 'fsdp'), 'head'), parts along dimension 0, may hold values from 0 to 0.8
- level_codes: int32 [16384, 18], P(('groups', 'seq', 'fsdp')), parts along dimension 0, may hold values from 0 to 255
- level_scale: float32 [18], replicated, may hold values from 0.05 to 1
- positions: int32 [16384], P(('groups', 'seq', 'fsdp')), parts along dimension 0, may hold values from 0 to 2047, as said below
- ssm_gain: float32 [2048], P('head'), may hold values from 0.25 to 1.75
Outputs:
- mixed_out: bfloat16 [16384, 2048], P(('groups', 'seq', 'fsdp'), 'head'), parts along dimension 0
The draws below stay inside these ranges and needn't reach their ends.
There are 2 independent parts, one for each index of `groups`. The reference program is written for one: setup_inputs(seed, part) draws one part's arguments, and reference() takes and returns one part's arrays. A program takes and returns all parts, laid end to end along the dimension named above; an argument that names none is the same for every part. Nothing has to cross between parts.
Inputs may be any that keep to these rules, and one draw needn't show every extreme that they name: positions[t] is 0 where a document begins (always at t = 0) and positions[t - 1] + 1 elsewhere.
All inputs are finite; a program needn't handle non-finite values.
Results may differ from the reference program's by a relative error of at most 0.008.
Values may be sent and summed in bfloat16 or wider, within the bound.
A program may use at most 64 MiB of HBM per device.

```python
import math
import jax
import jax.numpy as jnp
from jax import lax

D = 2048
ATT_HEADS = 16
SSM_HEADS = 32
HEAD_VALUES = 64
STATES = 128
WINDOW = 128
LEVELS = 18
TOK_DEV = 1024
TOKEN_TOTAL = 8192


def attention_pair(key):
    base_key = jax.random.fold_in(key, 501)
    key_collection = jax.random.split(base_key, 2)
    query_vals = jnp.clip(jax.random.normal(key_collection[0], (TOKEN_TOTAL, D), jnp.float32), -4.0, 4.0)
    key_vals = jnp.clip(jax.random.normal(key_collection[1], (TOKEN_TOTAL, D), jnp.float32), -4.0, 4.0)
    return (query_vals, key_vals)


def draw_query_rows(key, part):
    return attention_pair(key)[0].astype(jnp.bfloat16)


def draw_key_rows(key, part):
    return attention_pair(key)[1].astype(jnp.bfloat16)


def draw_decay_rate(key, part):
    base_key = jax.random.fold_in(key, 733)
    key_collection = jax.random.split(base_key, 9)
    fast_share = 0.5
    fast_heads = jax.random.uniform(key_collection[0], (SSM_HEADS,), jnp.float32) < fast_share
    fast_rate = jnp.exp(jax.random.uniform(key_collection[1], (SSM_HEADS,), jnp.float32, math.log(1.0 / 50.0), math.log(1.0 / 30.0)))
    slow_rate = jnp.exp(jax.random.uniform(key_collection[2], (SSM_HEADS,), jnp.float32, math.log(0.4), math.log(1.2))) / TOKEN_TOTAL
    head_decay_speed = jnp.where(fast_heads, fast_rate, slow_rate)
    block_total = TOKEN_TOTAL // TOK_DEV
    narrow_factor = jnp.exp(jax.random.uniform(key_collection[3], (block_total, SSM_HEADS), jnp.float32, math.log(0.5), math.log(2.0)))
    wide_factor = jnp.exp(jax.random.uniform(key_collection[7], (block_total, SSM_HEADS), jnp.float32, math.log(0.25), math.log(4.0)))
    block_multiplier = jnp.where(fast_heads[None, :], narrow_factor, wide_factor)
    block_multiplier = jnp.repeat(block_multiplier, TOK_DEV, axis=0)
    jaggedness = jax.random.uniform(key_collection[4], (TOKEN_TOTAL, SSM_HEADS), jnp.float32, 0.5, 1.5)
    leading_spike = jax.random.randint(key_collection[5], (1,), 0, TOKEN_TOTAL)
    trailing_spike = (leading_spike + 1 + jax.random.randint(key_collection[8], (1,), 0, TOKEN_TOTAL - 1)) % TOKEN_TOTAL
    spike_position = jnp.concatenate([leading_spike, trailing_spike])
    spike_length = jnp.concatenate([jnp.full((1,), math.log(2.0), jnp.float32), jax.random.uniform(key_collection[6], (1,), jnp.float32, 0.22, 0.69)])
    token_index = jnp.arange(TOKEN_TOTAL, dtype=jnp.int32)
    spike_events = jnp.sum(jnp.where(token_index[:, None] == spike_position[None, :], spike_length[None, :], 0.0), axis=1)
    return head_decay_speed[None, :] * block_multiplier * jaggedness + spike_events[:, None]


def draw_positions(key, part):
    base_key = jax.random.fold_in(key, 919)
    token_index = jnp.arange(TOKEN_TOTAL, dtype=jnp.int32)
    offset = TOK_DEV // 2
    random_marks = (jax.random.randint(base_key, (TOKEN_TOTAL,), 0, 2 * TOK_DEV) == 0) & (token_index >= offset + 2 * TOK_DEV)
    start_marks = random_marks | (token_index % (2 * TOK_DEV) == offset) | (token_index == 0)
    starts = jnp.where(start_marks, token_index, 0)
    return token_index - lax.cummax(starts, axis=0)


def touch_ends(entries, key, smallest, top_value):
    dims = entries.shape
    place = [jax.random.randint(jax.random.fold_in(key, axis), (), 0, dims[axis]) for axis in range(len(dims))]
    entries = entries.at[tuple(place)].set(smallest)
    longest = dims.index(max(dims))
    place[longest] = (place[longest] + 1) % dims[longest]
    return entries.at[tuple(place)].set(top_value)


def shard_levels(stream_key, shape, cuts, least, top_value):
    level = 1.0
    for dim, blocks in cuts:
        draws = jax.random.uniform(jax.random.fold_in(jax.random.fold_in(stream_key, 6), dim), (blocks,), jnp.float32, least / len(cuts), top_value / len(cuts))
        level = level * jnp.repeat(jnp.exp(draws), shape[dim] // blocks).reshape((-1,) + (1,) * (len(shape) - 1 - dim))
    return level


def normal_values(stream_key, dims, scale, most, cuts=(), kind=jnp.bfloat16):
    values = scale * jax.random.normal(stream_key, dims, jnp.float32)
    if cuts:
        values = values * shard_levels(stream_key, dims, cuts, -0.22, 0.18)
    return jnp.clip(values, -most, most).astype(kind)


def setup_inputs(seed: int = 0, part: int = 0) -> dict:
    keys = jax.random.split(jax.random.key(seed), 11)
    part_keys = jax.random.split(jax.random.fold_in(keys[10], part), 11)
    residual_in = normal_values(part_keys[0], (TOKEN_TOTAL, D), 1.0, 6.0, ((0, 8), (1, 2)))
    query_rows = draw_query_rows(jax.random.fold_in(jax.random.fold_in(keys[10], part), 71), part)
    key_rows = draw_key_rows(jax.random.fold_in(jax.random.fold_in(keys[10], part), 71), part)
    value_rows = normal_values(part_keys[3], (TOKEN_TOTAL, D), 1.0, 6.0, ((0, 8), (1, 2)))
    bc_weight = normal_values(keys[4], (D, 2 * STATES), D ** -0.5, 0.125, ((0, 4),))
    decay_rate = draw_decay_rate(jax.random.fold_in(jax.random.fold_in(keys[10], part), 71), part)
    level_codes = touch_ends(jax.random.randint(part_keys[6], (TOKEN_TOTAL, LEVELS), 0, 256), jax.random.fold_in(part_keys[6], 1), 0, 255).astype(jnp.int32)
    level_scale = jnp.clip(jnp.exp(jax.random.uniform(keys[7], (LEVELS,), jnp.float32, math.log(0.05), math.log(1.0))), 0.05, 1.0)
    positions = draw_positions(jax.random.fold_in(jax.random.fold_in(keys[10], part), 71), part)
    ssm_gain = jnp.clip(1.0 + 0.15 * jax.random.normal(keys[9], (D,), jnp.float32), 0.25, 1.75)
    return dict(residual_in=residual_in, query_rows=query_rows, key_rows=key_rows, value_rows=value_rows, bc_weight=bc_weight, decay_rate=decay_rate, level_codes=level_codes, level_scale=level_scale, positions=positions, ssm_gain=ssm_gain)


def attend_block(queries, keys_part, values_part, doc_pos, head_count):
    query_len = queries.shape[0]
    key_len = keys_part.shape[0]
    window_len = key_len - query_len
    shaped_q = queries.reshape(query_len, head_count, -1).astype(jnp.float32)
    shaped_k = keys_part.reshape(key_len, head_count, -1).astype(jnp.float32)
    shaped_v = values_part.reshape(key_len, head_count, -1).astype(jnp.float32)
    scores = jnp.einsum('qhd,khd->hqk', shaped_q, shaped_k) / math.sqrt(shaped_q.shape[2])
    query_idx = jnp.arange(query_len, dtype=jnp.int32)[:, None]
    key_idx = jnp.arange(key_len, dtype=jnp.int32)[None, :]
    distance = query_idx + window_len - key_idx
    visible = (distance >= 0) & (distance < window_len) & (distance <= doc_pos[:, None])
    masked = jnp.where(visible[None], scores, -jnp.inf)
    top_score = lax.optimization_barrier(jnp.max(masked, axis=2, keepdims=True))
    weights = jnp.exp(masked - top_score)
    probabilities = (weights / lax.optimization_barrier(jnp.sum(weights, axis=2, keepdims=True))).astype(jnp.bfloat16)
    return jnp.einsum('hqk,khd->qhd', probabilities.astype(jnp.float32), shaped_v).reshape(query_len, -1)

def reference(residual_in, query_rows, key_rows, value_rows, bc_weight, decay_rate, level_codes, level_scale, positions, ssm_gain):
    tokens, feature_count = residual_in.shape
    padding = jnp.zeros((WINDOW, feature_count), jnp.bfloat16)
    keys_all = jnp.concatenate([padding, key_rows], axis=0)
    values_all = jnp.concatenate([padding, value_rows], axis=0)

    def attend_at(index):
        start_row = index * WINDOW
        return attend_block(lax.dynamic_slice_in_dim(query_rows, start_row, WINDOW, 0), lax.dynamic_slice_in_dim(keys_all, start_row, 2 * WINDOW, 0), lax.dynamic_slice_in_dim(values_all, start_row, 2 * WINDOW, 0), lax.dynamic_slice_in_dim(positions, start_row, WINDOW, 0), ATT_HEADS)
    attended = lax.map(attend_at, jnp.arange(tokens // WINDOW, dtype=jnp.int32)).reshape(tokens, feature_count)
    hidden = (residual_in.astype(jnp.float32) + attended).astype(jnp.bfloat16)
    bc_full = jnp.dot(hidden, bc_weight, preferred_element_type=jnp.float32).astype(jnp.bfloat16)
    block_count = tokens // TOK_DEV
    b_blocks = bc_full[:, :STATES].reshape(block_count, TOK_DEV, STATES)
    c_blocks = bc_full[:, STATES:].reshape(block_count, TOK_DEV, STATES)
    values_h = hidden.reshape(block_count, TOK_DEV, SSM_HEADS, HEAD_VALUES)
    log_cum = -jnp.cumsum(decay_rate.reshape(block_count, TOK_DEV, SSM_HEADS), axis=1)
    log_end = log_cum[:, TOK_DEV - 1]
    scaled = (jnp.exp(log_end[:, None, :] - log_cum)[..., None] * values_h.astype(jnp.float32)).astype(jnp.bfloat16)
    states = jnp.einsum('jrn,jrhp->jnhp', b_blocks.astype(jnp.float32), scaled.astype(jnp.float32))
    prefix = jnp.cumsum(log_end, axis=0) - log_end
    span_log = prefix[:, None, :] - prefix[None, :, :] - log_end[None, :, :]
    block_idx = jnp.arange(block_count, dtype=jnp.int32)
    differ = jnp.bitwise_xor(block_idx[:, None], block_idx[None, :])
    cross_count = block_count.bit_length() - 1
    carried_list = []
    for bit_pos in range(cross_count):
        chosen = (block_idx[None, :] < block_idx[:, None]) & (differ >= 1 << bit_pos) & (differ < 2 << bit_pos)
        level_w = jnp.exp(jnp.where(chosen[:, :, None], span_log, -jnp.inf))
        carried_list.append(jnp.einsum('jih,inhp->jnhp', level_w, states, precision=lax.Precision.HIGHEST))
    carried = jnp.stack(carried_list, axis=1).astype(jnp.bfloat16)
    lambdas = (level_codes.astype(jnp.float32) * level_scale[None, :]).reshape(block_count, TOK_DEV, LEVELS)
    local_bits = TOK_DEV.bit_length() - 1
    token_index = jnp.arange(TOK_DEV, dtype=jnp.int32)
    xor_idx = jnp.bitwise_xor(token_index[:, None], token_index[None, :])
    causal = token_index[None, :] <= token_index[:, None]
    level_index = jnp.zeros((TOK_DEV, TOK_DEV), jnp.int32)
    for bit_pos in range(local_bits):
        level_index = level_index + (xor_idx >= 1 << bit_pos).astype(jnp.int32)

    def finish(operands):
        lam_blk, b_blk, c_blk, cum_blk, values_blk, carried_blk, hidden_blk = operands
        level_weight = jnp.take_along_axis(lam_blk, level_index, axis=1)
        gram_mat = jnp.dot(c_blk, b_blk.T, preferred_element_type=jnp.float32)
        shared = jnp.where(causal, gram_mat * level_weight, 0.0)
        cum_heads = cum_blk.T
        decay_mat = jnp.exp(jnp.where(causal[None], cum_heads[:, :, None] - cum_heads[:, None, :], -jnp.inf))
        mixing = (shared[None] * decay_mat).astype(jnp.bfloat16)
        intra_term = jnp.einsum('hts,shp->thp', mixing.astype(jnp.float32), values_blk.astype(jnp.float32))
        level_reads = jnp.einsum('rn,lnhp->rlhp', c_blk.astype(jnp.float32), carried_blk.astype(jnp.float32))
        lam_cross = lam_blk[:, local_bits + 1:local_bits + 1 + cross_count]
        cross_term = jnp.einsum('rl,rlhp->rhp', lam_cross, level_reads) * jnp.exp(cum_blk)[:, :, None]
        ssm_out = intra_term + cross_term
        inv_rms = lax.rsqrt(lax.optimization_barrier(jnp.mean(ssm_out * ssm_out, axis=2, keepdims=True)) + 1e-05)
        result = hidden_blk.astype(jnp.float32) + (ssm_out * inv_rms).reshape(TOK_DEV, -1) * ssm_gain[None, :]
        return result.astype(jnp.bfloat16)
    outputs = lax.map(finish, (lambdas, b_blocks, c_blocks, log_cum, values_h, carried, hidden.reshape(block_count, TOK_DEV, feature_count)))
    return outputs.reshape(tokens, feature_count)
```

```python
import functools
import math

import jax
import jax.numpy as jnp
from jax import lax
from jax.experimental import pallas as pl
from jax.experimental.pallas import tpu as pltpu
from jax.sharding import PartitionSpec as P

HEAD_DIM = 128
HEAD_VALUES = 64
STATES = 128
WINDOW = 128
CHUNK = 128
LOG2E = math.log2(math.e)
F32 = jnp.float32
BF16 = jnp.bfloat16
MESH = pl.DeviceIdType.MESH


def iota(shape, axis):
    return lax.broadcasted_iota(jnp.int32, shape, axis)


def dot(a, b):
    return jnp.dot(a, b, preferred_element_type=F32)


def dot_nt(a, b, precision=None):
    return lax.dot_general(a, b, (((1,), (1,)), ((), ())), precision=precision, preferred_element_type=F32)


def dot_tn(a, b):
    return lax.dot_general(a, b, (((0,), (0,)), ((), ())), preferred_element_type=F32)


def split2(x):
    hi = x.astype(BF16)
    lo = (x - hi.astype(F32)).astype(BF16)
    return jnp.concatenate([hi, lo], axis=1)


def plan(n):
    joins, reads = [], {}
    made = {}
    for i in range(n):
        for s in range(n.bit_length() - 1):
            if (i >> s) & 1:
                start = (i >> (s + 1)) << (s + 1)
                reads[i, s] = (start, start + (1 << s))
    def make(start, stop):
        if stop - start == 1 or (start, stop) in made:
            return
        mid = (start + stop) // 2
        make(start, mid)
        make(mid, stop)
        made[start, stop] = len(joins)
        joins.append((start, mid, stop))
    for i in range(n):
        for s in range(n.bit_length() - 1):
            if (i, s) in reads:
                make(*reads[i, s])
    return joins, made, reads


def mixer_kernel(
    head_bits, cross, seq_size,
    q_hbm, k_hbm, v_hbm, res_hbm, w_hbm, decay, codes, scale, pos, gain, out_hbm,
    q, k, v, res, w, hid, fu, sent, came, bc, state, raw, runs, y, ex, ef, lam, fac, spread, gone, gone_in,
    s_bf, s_in, carried, pay, outs,
    in_sem, kv_sem, w_sem, halo_send, halo_recv, wx_sem, gone_sem, bc_send, bc_recv, s_sem, z_send, z_recv,
    f_send, f_recv, out_sem,
):
    rows_total, width = q.shape
    n = rows_total // CHUNK
    ssm = decay.shape[0]
    inner = n.bit_length() - 1
    low_levels = CHUNK.bit_length()
    first_level = rows_total.bit_length()
    half = width // 2
    head_pos = lax.axis_index("head")
    z = lax.axis_index("seq")
    f = lax.axis_index("fsdp")
    sibling = {"fsdp": 1 - f}
    ahead = {"seq": z + 1}
    after = {"seq": z + f, "fsdp": 1 - f}
    has_next = z + 1 < seq_size
    has_prev = z > 0
    has_after = jnp.logical_or(f == 0, has_next)
    has_before = jnp.logical_or(f == 1, has_prev)

    def head_partner(bit):
        up = lax.rem(head_pos // (1 << bit), 2)
        return {"head": head_pos + (1 << bit) * (1 - 2 * up)}

    def rows_of(c):
        if isinstance(c, int):
            return pl.ds(c * CHUNK, CHUNK)
        return pl.ds(pl.multiple_of(c * CHUNK, CHUNK), CHUNK)

    def next_rows(c):
        if isinstance(c, int):
            return pl.ds((c + 1) * CHUNK, CHUNK)
        return pl.ds(pl.multiple_of((c + 1) * CHUNK, CHUNK), CHUNK)

    def load_k(c):
        return pltpu.make_async_copy(k_hbm.at[rows_of(c)], k.at[next_rows(c)], kv_sem.at[0, c])

    def load_v(c):
        return pltpu.make_async_copy(v_hbm.at[rows_of(c)], v.at[next_rows(c)], kv_sem.at[1, c])

    def load_q(c):
        return pltpu.make_async_copy(q_hbm.at[rows_of(c)], q.at[rows_of(c)], in_sem.at[0, c])

    def load_res(c):
        return pltpu.make_async_copy(res_hbm.at[rows_of(c)], res.at[rows_of(c)], in_sem.at[1, c])

    def remote(src, dst, send, recv, device):
        return pltpu.make_async_remote_copy(src, dst, send, recv, device_id=device, device_id_type=MESH)

    barrier = pltpu.get_barrier_semaphore()

    def greet(device):
        pl.semaphore_signal(barrier, inc=1, device_id=device, device_id_type=MESH)

    for bit in range(head_bits):
        greet(head_partner(bit))
    greet(sibling)

    @pl.when(has_next)
    def _():
        greet(ahead)

    @pl.when(has_prev)
    def _():
        greet({"seq": z - 1})

    @pl.when(jnp.logical_and(f == 1, has_next))
    def _():
        greet(after)

    @pl.when(jnp.logical_and(f == 0, has_prev))
    def _():
        greet({"seq": z - 1, "fsdp": 1 - f})

    load_k(0).start()
    load_v(0).start()
    order = [(i + 1) % n for i in range(n)]
    for c in order:
        if c:
            load_k(c).start()
            load_v(c).start()
        load_q(c).start()
        load_res(c).start()
    depth = w_hbm.shape[0]
    own_rows = pl.ds(pl.multiple_of(f * depth, depth), depth)
    w_load = pltpu.make_async_copy(w_hbm, w.at[own_rows], w_sem)
    w_load.start()

    @pl.when(jnp.logical_not(has_before))
    def _():
        k[:CHUNK, :] = jnp.zeros((CHUNK, width), BF16)
        v[:CHUNK, :] = jnp.zeros((CHUNK, width), BF16)

    tri = jnp.where(iota((CHUNK, CHUNK), 1) <= iota((CHUNK, CHUNK), 0), 1.0, 0.0)
    decays = decay[...] * LOG2E
    stacked = jnp.concatenate([decays[:, c * CHUNK : (c + 1) * CHUNK] for c in range(n)], axis=0)
    sums = dot_nt(tri, stacked, lax.Precision.HIGHEST)
    total = sums[CHUNK - 1 :, :]
    rise = split2(jnp.exp2(0.5 * total - sums))
    fall = split2(jnp.exp2(sums - 0.5 * total))
    for c in range(n):
        parts = [side[:, a * n * ssm + c * ssm : a * n * ssm + (c + 1) * ssm] for side in (rise, fall) for a in range(2)]
        ef[c] = jnp.concatenate(parts, axis=1)
    tot = [total[:, c * ssm : (c + 1) * ssm] for c in range(n)]
    joins, made, reads = plan(n)

    def between(start, stop):
        return functools.reduce(lambda a, b: a + b, tot[start:stop], jnp.zeros_like(tot[0]))

    table = []

    def put(exponent):
        table.append(exponent)
        return len(table) - 1

    for c in range(n):
        put(0.5 * tot[c] + between(c + 1, n))
    for c in range(n):
        put(0.5 * tot[c] + between(0, c))
    all_row = put(between(0, n))

    def own_half(start, stop):
        return 0.5 * tot[start] if stop - start == 1 else jnp.zeros_like(tot[0])

    join_rows = [
        (put(own_half(start, mid) + between(mid, stop)), put(own_half(mid, stop))) for start, mid, stop in joins
    ]
    read_rows = {
        (i, s): put(own_half(*reads[i, s]) + between(reads[i, s][1], i) + 0.5 * tot[i]) for (i, s) in sorted(reads)
    }
    while len(table) % 16:
        put(jnp.zeros_like(tot[0]))
    same = lax.rem(iota((2 * ssm, width), 0), ssm) == iota((2 * ssm, width), 1) // HEAD_VALUES
    spread[...] = jnp.where(same, 1.0, 0.0).astype(BF16)
    fac[...] = dot(split2(jnp.exp2(-jnp.concatenate(table, axis=0))), spread[...])
    gone[...] = jnp.broadcast_to(fac[all_row : all_row + 1, :], gone.shape)
    eye = jnp.where(iota((CHUNK, CHUNK), 1) == iota((CHUNK, CHUNK), 0), 1.0, 0.0).astype(BF16)
    for c in range(n):
        code = codes[:, c * CHUNK : (c + 1) * CHUNK].astype(F32).astype(BF16)
        lam[c] = dot_nt(eye, code) * scale[...]

    links = head_bits + 1
    links += has_next.astype(jnp.int32) + has_prev.astype(jnp.int32)
    links += jnp.logical_and(f == 1, has_next).astype(jnp.int32) + jnp.logical_and(f == 0, has_prev).astype(jnp.int32)
    pl.semaphore_wait(barrier, links)
    w_send = remote(w_hbm, w.at[own_rows], wx_sem.at[0], wx_sem.at[1], sibling)
    w_send.start()
    tail = pl.ds(rows_total - WINDOW, WINDOW)
    halo = [
        remote(k_hbm.at[tail], k.at[pl.ds(0, WINDOW)], halo_send.at[0], halo_recv.at[0], after),
        remote(v_hbm.at[tail], v.at[pl.ds(0, WINDOW)], halo_send.at[1], halo_recv.at[1], after),
    ]

    @pl.when(has_after)
    def _():
        for copy in halo:
            copy.start()

    gone_send = remote(gone, gone_in, gone_sem.at[0], gone_sem.at[1], sibling)
    gone_send.start()

    def bc_copy(bit, c):
        return remote(
            sent.at[bit, rows_of(c)], came.at[bit, rows_of(c)], bc_send.at[bit, c], bc_recv.at[bit, c], head_partner(bit)
        )

    load_k(0).wait()
    load_v(0).wait()
    w_load.wait()
    w_send.wait()
    near = (iota((CHUNK, CHUNK), 0) - iota((CHUNK, CHUNK), 1)).astype(F32)
    far = near + float(WINDOW)
    factor = LOG2E / math.sqrt(HEAD_DIM)

    def attend(i, carry):
        c = lax.rem(i + 1, n)

        @pl.when(i < n - 1)
        def _():
            load_k(c).wait()
            load_v(c).wait()

        @pl.when(jnp.logical_and(i == n - 1, has_before))
        def _():
            for copy in halo:
                copy.wait_recv()

        load_q(c).wait()
        load_res(c).wait()
        rows = rows_of(c)
        both = pl.ds(pl.multiple_of(c * CHUNK, CHUNK), 2 * CHUNK)
        pos_col = jnp.broadcast_to(pos[c].astype(F32), (CHUNK, CHUNK)).T
        mask_cur = jnp.where((near >= 0) & (near <= pos_col), 0.0, -jnp.inf)
        mask_prev = jnp.where((far < float(WINDOW)) & (far <= pos_col), 0.0, -jnp.inf)
        mask = jnp.concatenate([mask_prev, mask_cur], axis=1)
        heads = [slice(h * HEAD_DIM, (h + 1) * HEAD_DIM) for h in range(width // HEAD_DIM)]
        scores = [dot_nt(q[rows, cols], k[both, cols]) + mask for cols in heads]
        tops = [jnp.max(s, axis=1, keepdims=True) for s in scores]
        raised = [jnp.exp2((s - top) * factor) for s, top in zip(scores, tops)]
        totals = [jnp.sum(e, axis=1, keepdims=True) for e in raised]
        weighted = [dot(e.astype(BF16), v[both, cols]) for e, cols in zip(raised, heads)]
        hidden = jnp.concatenate(
            [
                (res[rows, cols].astype(F32) + a * (1.0 / t)).astype(BF16)
                for cols, a, t in zip(heads, weighted, totals)
            ],
            axis=1,
        )
        hid[rows, :] = hidden
        sent[0, rows, :] = dot(hidden, w[...]).astype(BF16)
        if head_bits:
            bc_copy(0, c).start()
        fu[rows, :] = (dot(ef[c][:, 2 * ssm :], spread[...]) * hidden.astype(F32)).astype(BF16)
        return carry

    lax.fori_loop(0, n, attend, 0)

    state[...] = jnp.zeros_like(state)

    def collect(i, carry):
        c = lax.rem(i + 1, n)
        rows = rows_of(c)
        both = sent[0, rows, :]
        for bit in range(head_bits):
            bc_copy(bit, c).wait_recv()
            both = (sent[bit, rows, :].astype(F32) + came[bit, rows, :].astype(F32)).astype(BF16)
            if bit < head_bits - 1:
                sent[bit + 1, rows, :] = both
                bc_copy(bit + 1, c).start()
        bc[rows, :] = both
        chunk = dot_tn(both[:, :STATES], fu[rows, :])
        raw[c] = chunk
        state[...] += chunk * fac[pl.ds(c, 1), :]
        return carry

    lax.fori_loop(0, n, collect, 0)
    s_bf[...] = state[...].astype(BF16)
    s_send = remote(s_bf, s_in, s_sem.at[0], s_sem.at[1], sibling)
    s_send.start()

    side = (CHUNK, CHUNK)
    differ = iota(side, 0) ^ iota(side, 1)
    causal = iota(side, 1) <= iota(side, 0)

    def run_of(start, stop):
        return raw[start] if stop - start == 1 else runs[made[start, stop]]

    def local(i):
        rows = rows_of(i)
        for number, (start, mid, stop) in enumerate(joins):
            if stop == i:
                one, two = join_rows[number]
                runs[number] = run_of(start, mid) * fac[one : one + 1, :] + run_of(mid, stop) * fac[two : two + 1, :]
        lam_c = lam[i]
        weight = jnp.broadcast_to(lam_c[:, 0:1], side)
        for level in range(1, low_levels):
            weight = jnp.where(differ >= 1 << level - 1, lam_c[:, level : level + 1], weight)
        b, c = bc[rows, :STATES], bc[rows, STATES:]
        shared = jnp.where(causal, dot_nt(c, b) * weight, 0.0)
        left = [shared.astype(BF16)]
        right = [fu[rows, :]]
        c32 = c.astype(F32)
        for s in range(inner):
            if (i, s) in reads:
                row = read_rows[i, s]
                left.append((c32 * lam_c[:, low_levels + s : low_levels + s + 1]).astype(BF16))
                right.append((run_of(*reads[i, s]) * fac[row : row + 1, :]).astype(BF16))
        terms = dot(jnp.concatenate(left, axis=1), jnp.concatenate(right, axis=0))
        grow = dot(ef[i][:, : 2 * ssm], spread[...])
        y[rows, :] = terms * grow
        ex[rows, :] = grow * fac[n + i : n + i + 1, :]

    done = 0

    def locals_until(stop):
        nonlocal done
        while done < min(stop, n):
            local(done)
            done += 1

    gone_send.wait()
    own_cols = pl.ds(pl.multiple_of(f * half, half), half)
    other_cols = pl.ds(pl.multiple_of((1 - f) * half, half), half)
    first_core = f == 0

    def z_copy(level):
        return remote(
            pay.at[level], carried.at[level, :, own_cols], z_send.at[level], z_recv.at[level], ahead
        )

    def forward(level):
        return remote(
            carried.at[level, :, own_cols], carried.at[level, :, own_cols], f_send.at[level], f_recv.at[level], sibling
        )

    def bit_of(x, level):
        return lax.rem(x // (1 << level - 1), 2) == 1

    def takes(level):
        return bit_of(z, level)

    def gives(level):
        return jnp.logical_and(has_next, bit_of(z + 1, level))

    locals_until(2)
    s_send.wait()
    mine = gone[0:1, :]
    theirs = gone_in[0:1, :]
    gone_last = jnp.where(first_core, theirs, mine)
    gone_chip = mine * theirs
    mine_s = state[...]
    theirs_s = s_in[...].astype(F32)
    carried[0] = jnp.where(first_core, 0.0, theirs_s).astype(BF16)
    chip = jnp.where(first_core, mine_s, theirs_s) * gone_last + jnp.where(first_core, theirs_s, mine_s)
    acc = state
    acc[...] = chip
    gone[0:1, :] = gone_chip
    own_gone = gone[0:1, own_cols]
    for level in range(1, cross):

        @pl.when(jnp.logical_not(takes(level)))
        def _():
            carried[level] = jnp.zeros((STATES, width), BF16)

            @pl.when(gives(level))
            def _():
                pay[level] = acc[:, own_cols].astype(BF16)
                z_copy(level).start()

        locals_until(2 + level * 3)

        @pl.when(takes(level))
        def _():
            z_copy(level).wait_recv()
            forward(level).start()
            moved = carried[level, :, own_cols].astype(F32) * own_gone

            @pl.when(gives(level))
            def _():
                pay[level] = moved.astype(BF16)
                z_copy(level).start()

            acc[:, own_cols] += moved

    locals_until(n)
    first_gone = jnp.where(first_core, 1.0, theirs)
    for level in range(1, cross):

        @pl.when(takes(level))
        def _():
            forward(level).wait()
            carried[level] = (carried[level].astype(F32) * first_gone).astype(BF16)

    tile = min(2 * CHUNK, width)
    group = jnp.where(
        iota((tile, tile), 0) // HEAD_VALUES == iota((tile, tile), 1) // HEAD_VALUES, 1.0 / HEAD_VALUES, 0.0
    ).astype(BF16)
    tiles = [slice(g * tile, (g + 1) * tile) for g in range(width // tile)]

    def store(c):
        return pltpu.make_async_copy(outs.at[rows_of(c)], out_hbm.at[rows_of(c)], out_sem.at[c])

    def finish(c, carry):
        rows = rows_of(c)
        lam_c = lam[c]
        c32 = bc[rows, STATES:].astype(F32)
        read = jnp.concatenate(
            [(c32 * lam_c[:, first_level + s : first_level + s + 1]).astype(BF16) for s in range(cross)], axis=1
        )
        held = carried[...].reshape(cross * STATES, width)
        terms = [y[rows, cols] + dot(read, held[:, cols]) * ex[rows, cols] for cols in tiles]
        means = [dot((term * term).astype(BF16), group) for term in terms]
        for cols, term, mean in zip(tiles, terms, means):
            outs[rows, cols] = (
                hid[rows, cols].astype(F32) + term * lax.rsqrt(mean + 1e-05) * gain[:, cols]
            ).astype(BF16)
        store(c).start()
        return carry

    lax.fori_loop(0, n, finish, 0)

    @pl.when(has_after)
    def _():
        for copy in halo:
            copy.wait_send()

    for bit in range(head_bits):
        for c in range(n):
            bc_copy(bit, c).wait_send()
    for level in range(1, cross):

        @pl.when(gives(level))
        def _():
            z_copy(level).wait_send()

    for c in range(n):
        store(c).wait()


def body(
    residual_in,
    query_rows,
    key_rows,
    value_rows,
    bc_weight,
    decay_rate,
    level_codes,
    level_scale,
    positions,
    ssm_gain,
):
    rows, width = residual_in.shape
    n = rows // CHUNK
    ssm = decay_rate.shape[1]
    seq_size = lax.axis_size("seq")
    head_bits = lax.axis_size("head").bit_length() - 1
    cross = (seq_size * lax.axis_size("fsdp")).bit_length() - 1
    bits = max(head_bits, 1)
    joins, _, reads = plan(n)
    factors = 2 * n + 1 + 2 * len(joins) + len(reads)
    factors += -factors % 16
    dma = pltpu.SemaphoreType.DMA
    any_spec = pl.BlockSpec(memory_space=pl.ANY)
    vmem_spec = pl.BlockSpec(memory_space=pltpu.VMEM)
    scratch = [
        pltpu.VMEM((rows, width), BF16),
        pltpu.VMEM((rows + CHUNK, width), BF16),
        pltpu.VMEM((rows + CHUNK, width), BF16),
        pltpu.VMEM((rows, width), BF16),
        pltpu.VMEM((2 * bc_weight.shape[0], bc_weight.shape[1]), BF16),
        pltpu.VMEM((rows, width), BF16),
        pltpu.VMEM((rows, width), BF16),
        pltpu.VMEM((bits, rows, 2 * STATES), BF16),
        pltpu.VMEM((bits, rows, 2 * STATES), BF16),
        pltpu.VMEM((rows, 2 * STATES), BF16),
        pltpu.VMEM((STATES, width), F32),
        pltpu.VMEM((n, STATES, width), F32),
        pltpu.VMEM((len(joins), STATES, width), F32),
        pltpu.VMEM((rows, width), F32),
        pltpu.VMEM((rows, width), F32),
        pltpu.VMEM((n, CHUNK, 4 * ssm), BF16),
        pltpu.VMEM((n, CHUNK, level_codes.shape[1]), F32),
        pltpu.VMEM((factors, width), F32),
        pltpu.VMEM((2 * ssm, width), BF16),
        pltpu.VMEM((8, width), F32),
        pltpu.VMEM((8, width), F32),
        pltpu.VMEM((STATES, width), BF16),
        pltpu.VMEM((STATES, width), BF16),
        pltpu.VMEM((cross, STATES, width), BF16),
        pltpu.VMEM((cross, STATES, width // 2), BF16),
        pltpu.VMEM((rows, width), BF16),
        dma((2, n)), dma((2, n)), dma, dma((2,)), dma((2,)), dma((2,)), dma((2,)), dma((bits, n)), dma((bits, n)),
        dma((2,)), dma((cross,)), dma((cross,)), dma((cross,)), dma((cross,)), dma((n,)),
    ]
    return pl.pallas_call(
        functools.partial(mixer_kernel, head_bits, cross, seq_size),
        in_specs=[any_spec] * 5 + [vmem_spec] * 5,
        out_specs=any_spec,
        out_shape=jax.ShapeDtypeStruct((rows, width), BF16),
        scratch_shapes=scratch,
        name="attend_and_mix",
        compiler_params=pltpu.CompilerParams(collective_id=0, has_side_effects=True, vmem_limit_bytes=56 * 2**20),
        cost_estimate=pl.CostEstimate(flops=rows * width * 8000, bytes_accessed=12 * rows * width, transcendentals=0),
    )(
        query_rows, key_rows, value_rows, residual_in, bc_weight, decay_rate.T, level_codes.T, level_scale[None, :],
        positions.reshape(n, 1, CHUNK), ssm_gain[None, :],
    )


def solution(mesh):
    in_specs = (
        P(("groups", "seq", "fsdp"), "head"),
        P(("groups", "seq", "fsdp"), "head"),
        P(("groups", "seq", "fsdp"), "head"),
        P(("groups", "seq", "fsdp"), "head"),
        P(("head", "fsdp"), None),
        P(("groups", "seq", "fsdp"), "head"),
        P(("groups", "seq", "fsdp"), None),
        P(),
        P(("groups", "seq", "fsdp")),
        P("head"),
    )
    out_specs = P(("groups", "seq", "fsdp"), "head")
    return jax.shard_map(body, mesh=mesh, in_specs=in_specs, out_specs=out_specs, check_vma=False)
```

```python
import functools
import math

import jax
import jax.numpy as jnp
from jax import lax
from jax.experimental import pallas as pl
from jax.experimental.pallas import tpu as pltpu
from jax.sharding import PartitionSpec as P

HEAD_DIM = 128
HEAD_VALUES = 64
STATES = 128
WINDOW = 128
CHUNK = 128
LOG2E = math.log2(math.e)
F32 = jnp.float32
BF16 = jnp.bfloat16
MESH = pl.DeviceIdType.MESH
PIECE = 256


def iota(shape, axis):
    return lax.broadcasted_iota(jnp.int32, shape, axis)


def dot(a, b):
    return jnp.dot(a, b, preferred_element_type=F32)


def dot_nt(a, b, precision=None):
    return lax.dot_general(a, b, (((1,), (1,)), ((), ())), precision=precision, preferred_element_type=F32)


def dot_tn(a, b):
    return lax.dot_general(a, b, (((0,), (0,)), ((), ())), preferred_element_type=F32)


def split2(x):
    hi = x.astype(BF16)
    lo = (x - hi.astype(F32)).astype(BF16)
    return jnp.concatenate([hi, lo], axis=1)


def plan(n):
    joins, reads = [], {}
    made = {}
    for i in range(n):
        for s in range(n.bit_length() - 1):
            if (i >> s) & 1:
                start = (i >> (s + 1)) << (s + 1)
                reads[i, s] = (start, start + (1 << s))
    def make(start, stop):
        if stop - start == 1 or (start, stop) in made:
            return
        mid = (start + stop) // 2
        make(start, mid)
        make(mid, stop)
        made[start, stop] = len(joins)
        joins.append((start, mid, stop))
    for i in range(n):
        for s in range(n.bit_length() - 1):
            if (i, s) in reads:
                make(*reads[i, s])
    return joins, made, reads


def mixer_kernel(
    head_bits, cross, seq_size,
    q_hbm, k_hbm, v_hbm, res_hbm, w_hbm, decay_hbm, codes_hbm, scale_hbm, pos_hbm, gain_hbm, out,
    q, k, v, res, w, decay, codes, scale, pos, gain, hid, fu, sent, came, b_all, reads_all, state, raw, runs, y, ex, ef,
    lam, fac, spread, gone, gone_in, s_bf, s_in, carried, pay,
    small_sem, in_sem, kv_sem, w_sem, halo_send, halo_recv, wx_sem, gone_sem, bc_send, bc_recv, s_send, s_recv,
    z_send, z_recv, f_send, f_recv,
):
    rows_total, width = q.shape
    n = rows_total // CHUNK
    ssm = decay.shape[0]
    inner = n.bit_length() - 1
    low_levels = CHUNK.bit_length()
    first_level = rows_total.bit_length()
    half = width // 2
    head_pos = lax.axis_index("head")
    z = lax.axis_index("seq")
    f = lax.axis_index("fsdp")
    sibling = {"fsdp": 1 - f}
    ahead = {"seq": z + 1}
    after = {"seq": z + f, "fsdp": 1 - f}
    has_next = z + 1 < seq_size
    has_prev = z > 0
    has_after = jnp.logical_or(f == 0, has_next)
    has_before = jnp.logical_or(f == 1, has_prev)

    def head_partner(bit):
        up = lax.rem(head_pos // (1 << bit), 2)
        return {"head": head_pos + (1 << bit) * (1 - 2 * up)}

    def rows_of(c):
        if isinstance(c, int):
            return pl.ds(c * CHUNK, CHUNK)
        return pl.ds(pl.multiple_of(c * CHUNK, CHUNK), CHUNK)

    def next_rows(c):
        if isinstance(c, int):
            return pl.ds((c + 1) * CHUNK, CHUNK)
        return pl.ds(pl.multiple_of((c + 1) * CHUNK, CHUNK), CHUNK)

    def load_k(c):
        return pltpu.make_async_copy(k_hbm.at[rows_of(c)], k.at[next_rows(c)], kv_sem.at[0, c])

    def load_v(c):
        return pltpu.make_async_copy(v_hbm.at[rows_of(c)], v.at[next_rows(c)], kv_sem.at[1, c])

    def load_q(c):
        return pltpu.make_async_copy(q_hbm.at[rows_of(c)], q.at[rows_of(c)], in_sem.at[0, c])

    def load_res(c):
        return pltpu.make_async_copy(res_hbm.at[rows_of(c)], res.at[rows_of(c)], in_sem.at[1, c])

    def remote(src, dst, send, recv, device):
        return pltpu.make_async_remote_copy(src, dst, send, recv, device_id=device, device_id_type=MESH)

    barrier = pltpu.get_barrier_semaphore()

    def greet(device):
        pl.semaphore_signal(barrier, inc=1, device_id=device, device_id_type=MESH)

    for bit in range(head_bits):
        greet(head_partner(bit))
    greet(sibling)

    @pl.when(has_next)
    def _():
        greet(ahead)

    @pl.when(has_prev)
    def _():
        greet({"seq": z - 1})

    @pl.when(jnp.logical_and(f == 1, has_next))
    def _():
        greet(after)

    @pl.when(jnp.logical_and(f == 0, has_prev))
    def _():
        greet({"seq": z - 1, "fsdp": 1 - f})

    smalls = [
        pltpu.make_async_copy(src, dst, small_sem.at[number])
        for number, (src, dst) in enumerate(
            [(decay_hbm, decay), (codes_hbm, codes), (scale_hbm, scale), (pos_hbm, pos), (gain_hbm, gain)]
        )
    ]
    for copy in smalls:
        copy.start()
    depth = w_hbm.shape[0]
    own_rows = pl.ds(pl.multiple_of(f * depth, depth), depth)
    w_load = pltpu.make_async_copy(w_hbm, w.at[own_rows], w_sem)
    w_load.start()
    load_k(0).start()
    load_v(0).start()
    order = [(i + 1) % n for i in range(n)]
    for c in order:
        if c:
            load_k(c).start()
            load_v(c).start()
        load_q(c).start()
        load_res(c).start()

    @pl.when(jnp.logical_not(has_before))
    def _():
        k[:CHUNK, :] = jnp.zeros((CHUNK, width), BF16)
        v[:CHUNK, :] = jnp.zeros((CHUNK, width), BF16)

    links = head_bits + 1
    links += has_next.astype(jnp.int32) + has_prev.astype(jnp.int32)
    links += jnp.logical_and(f == 1, has_next).astype(jnp.int32) + jnp.logical_and(f == 0, has_prev).astype(jnp.int32)
    pl.semaphore_wait(barrier, links)
    tail = pl.ds(rows_total - WINDOW, WINDOW)
    halo = [
        remote(k_hbm.at[tail], k.at[pl.ds(0, WINDOW)], halo_send.at[0], halo_recv.at[0], after),
        remote(v_hbm.at[tail], v.at[pl.ds(0, WINDOW)], halo_send.at[1], halo_recv.at[1], after),
    ]

    @pl.when(has_after)
    def _():
        for copy in halo:
            copy.start()

    w_send = remote(w_hbm, w.at[own_rows], wx_sem.at[0], wx_sem.at[1], sibling)
    w_send.start()
    for copy in smalls:
        copy.wait()

    tri = jnp.where(iota((CHUNK, CHUNK), 1) <= iota((CHUNK, CHUNK), 0), 1.0, 0.0)
    decays = decay[...] * LOG2E
    stacked = jnp.concatenate([decays[:, c * CHUNK : (c + 1) * CHUNK] for c in range(n)], axis=0)
    sums = dot_nt(tri, stacked, lax.Precision.HIGHEST)
    total = sums[CHUNK - 1 :, :]
    rise = split2(jnp.exp2(0.5 * total - sums))
    fall = split2(jnp.exp2(sums - 0.5 * total))
    for c in range(n):
        parts = [side[:, a * n * ssm + c * ssm : a * n * ssm + (c + 1) * ssm] for side in (rise, fall) for a in range(2)]
        ef[c] = jnp.concatenate(parts, axis=1)
    tot = [total[:, c * ssm : (c + 1) * ssm] for c in range(n)]
    joins, made, reads = plan(n)

    def between(start, stop):
        return functools.reduce(lambda a, b: a + b, tot[start:stop], jnp.zeros_like(tot[0]))

    table = []

    def put(exponent):
        table.append(exponent)
        return len(table) - 1

    for c in range(n):
        put(0.5 * tot[c] + between(c + 1, n))
    for c in range(n):
        put(0.5 * tot[c] + between(0, c))
    all_row = put(between(0, n))

    def own_half(start, stop):
        return 0.5 * tot[start] if stop - start == 1 else jnp.zeros_like(tot[0])

    join_rows = [
        (put(own_half(start, mid) + between(mid, stop)), put(own_half(mid, stop))) for start, mid, stop in joins
    ]
    read_rows = {
        (i, s): put(own_half(*reads[i, s]) + between(reads[i, s][1], i) + 0.5 * tot[i]) for (i, s) in sorted(reads)
    }
    while len(table) % 16:
        put(jnp.zeros_like(tot[0]))
    same = lax.rem(iota((2 * ssm, width), 0), ssm) == iota((2 * ssm, width), 1) // HEAD_VALUES
    spread[...] = jnp.where(same, 1.0, 0.0).astype(BF16)
    fac[...] = dot(split2(jnp.exp2(-jnp.concatenate(table, axis=0))), spread[...])
    gone[...] = jnp.broadcast_to(fac[all_row : all_row + 1, :], gone.shape)
    eye = jnp.where(iota((CHUNK, CHUNK), 1) == iota((CHUNK, CHUNK), 0), 1.0, 0.0).astype(BF16)
    for c in range(n):
        code = codes[:, c * CHUNK : (c + 1) * CHUNK].astype(F32).astype(BF16)
        lam[c] = dot_nt(eye, code) * scale[...]

    gone_send = remote(gone, gone_in, gone_sem.at[0], gone_sem.at[1], sibling)
    gone_send.start()

    def bc_copy(kind, bit, c):
        return remote(
            sent.at[kind, bit, rows_of(c)], came.at[kind, bit, rows_of(c)], bc_send.at[kind, bit, c],
            bc_recv.at[kind, bit, c], head_partner(bit),
        )

    def summed(kind, c):
        rows = rows_of(c)
        value = sent[kind, 0, rows, :]
        for bit in range(head_bits):
            bc_copy(kind, bit, c).wait_recv()
            value = (sent[kind, bit, rows, :].astype(F32) + came[kind, bit, rows, :].astype(F32)).astype(BF16)
            if bit < head_bits - 1:
                sent[kind, bit + 1, rows, :] = value
                bc_copy(kind, bit + 1, c).start()
        return value

    def collect(c):
        rows = rows_of(c)
        b = summed(0, c)
        b_all[rows, :] = b
        chunk = dot_tn(b, fu[rows, :])
        raw[c] = chunk
        state[...] += chunk * fac[pl.ds(c, 1), :]

    state[...] = jnp.zeros_like(state)

    load_k(0).wait()
    load_v(0).wait()
    w_load.wait()
    w_send.wait()
    near = (iota((CHUNK, CHUNK), 0) - iota((CHUNK, CHUNK), 1)).astype(F32)
    far = near + float(WINDOW)
    factor = LOG2E / math.sqrt(HEAD_DIM)

    def attend(i, carry):
        c = lax.rem(i + 1, n)

        @pl.when(i < n - 1)
        def _():
            load_k(c).wait()
            load_v(c).wait()

        @pl.when(jnp.logical_and(i == n - 1, has_before))
        def _():
            for copy in halo:
                copy.wait_recv()

        load_q(c).wait()
        load_res(c).wait()
        rows = rows_of(c)
        both = pl.ds(pl.multiple_of(c * CHUNK, CHUNK), 2 * CHUNK)
        pos_col = jnp.broadcast_to(pos[c].astype(F32), (CHUNK, CHUNK)).T
        mask_cur = jnp.where((near >= 0) & (near <= pos_col), 0.0, -jnp.inf)
        mask_prev = jnp.where((far < float(WINDOW)) & (far <= pos_col), 0.0, -jnp.inf)
        mask = jnp.concatenate([mask_prev, mask_cur], axis=1)
        heads = [slice(h * HEAD_DIM, (h + 1) * HEAD_DIM) for h in range(width // HEAD_DIM)]
        scores = [dot_nt(q[rows, cols], k[both, cols]) + mask for cols in heads]
        tops = [jnp.max(s, axis=1, keepdims=True) for s in scores]
        raised = [jnp.exp2((s - top) * factor) for s, top in zip(scores, tops)]
        totals = [jnp.sum(e, axis=1, keepdims=True) for e in raised]
        weighted = [dot(e.astype(BF16), v[both, cols]) for e, cols in zip(raised, heads)]
        hidden = jnp.concatenate(
            [
                (res[rows, cols].astype(F32) + a * (1.0 / t)).astype(BF16)
                for cols, a, t in zip(heads, weighted, totals)
            ],
            axis=1,
        )
        hid[rows, :] = hidden
        part = dot(hidden, w[...]).astype(BF16)
        sent[0, 0, rows, :] = part[:, :STATES]
        sent[1, 0, rows, :] = part[:, STATES:]
        if head_bits:
            bc_copy(0, 0, c).start()
        fu[rows, :] = (dot(ef[c][:, 2 * ssm :], spread[...]) * hidden.astype(F32)).astype(BF16)
        return carry

    lax.fori_loop(0, n, attend, 0)

    if head_bits:
        for number in range(n):
            bc_copy(1, 0, order[number]).start()
    for number in range(n):
        collect(order[number])

    pieces = half // PIECE if half % PIECE == 0 else 1
    step = half // pieces

    def own_piece(p):
        return pl.ds(pl.multiple_of(f * half + p * step, step), step)

    def other_piece(p):
        return pl.ds(pl.multiple_of((1 - f) * half + p * step, step), step)

    def s_copy(p):
        cols = other_piece(p)
        return remote(s_bf.at[:, cols], s_in.at[:, cols], s_send.at[p], s_recv.at[p], sibling)

    own_cols = pl.ds(pl.multiple_of(f * half, half), half)
    rest = remote(s_bf.at[:, own_cols], s_in.at[:, own_cols], s_send.at[pieces], s_recv.at[pieces], sibling)
    first_core = f == 0
    for p in range(pieces):
        s_bf[:, other_piece(p)] = state[:, other_piece(p)].astype(BF16)
        s_copy(p).start()
    s_bf[:, own_cols] = state[:, own_cols].astype(BF16)

    @pl.when(first_core)
    def _():
        rest.start()

    side = (CHUNK, CHUNK)
    differ = iota(side, 0) ^ iota(side, 1)
    causal = iota(side, 1) <= iota(side, 0)

    def run_of(start, stop):
        return raw[start] if stop - start == 1 else runs[made[start, stop]]

    def local(i):
        rows = rows_of(i)
        lam_c = lam[i]
        weight = jnp.broadcast_to(lam_c[:, 0:1], side)
        for level in range(1, low_levels):
            weight = jnp.where(differ >= 1 << level - 1, lam_c[:, level : level + 1], weight)
        b, c = b_all[rows, :], summed(1, i)
        shared = jnp.where(causal, dot_nt(c, b) * weight, 0.0)
        left = [shared.astype(BF16)]
        right = [fu[rows, :]]
        c32 = c.astype(F32)
        for s in range(inner):
            if (i, s) in reads:
                row = read_rows[i, s]
                left.append((c32 * lam_c[:, low_levels + s : low_levels + s + 1]).astype(BF16))
                right.append((run_of(*reads[i, s]) * fac[row : row + 1, :]).astype(BF16))
        for s in range(cross):
            reads_all[rows, s * STATES : (s + 1) * STATES] = (
                c32 * lam_c[:, first_level + s : first_level + s + 1]
            ).astype(BF16)
        terms = dot(jnp.concatenate(left, axis=1), jnp.concatenate(right, axis=0))
        grow = dot(ef[i][:, : 2 * ssm], spread[...])
        y[rows, :] = terms * grow
        ex[rows, :] = grow * fac[n + i : n + i + 1, :]

    gone_send.wait()
    mine = gone[0:1, :]
    theirs = gone_in[0:1, :]
    gone_last = jnp.where(first_core, theirs, mine)
    gone_in[1:2, :] = gone_last
    gone_in[2:3, :] = mine * theirs
    gone_in[3:4, :] = jnp.where(first_core, 1.0, theirs)

    def z_copy(level, p):
        return remote(
            pay.at[level, :, pl.ds(p * step, step)], carried.at[level, :, own_piece(p)], z_send.at[level, p],
            z_recv.at[level, p], ahead,
        )

    def forward(level, p):
        cols = own_piece(p)
        return remote(
            carried.at[level, :, cols], carried.at[level, :, cols], f_send.at[level, p], f_recv.at[level, p], sibling
        )

    def bit_of(x, level):
        return lax.rem(x // (1 << level - 1), 2) == 1

    def takes(level):
        return bit_of(z, level)

    def gives(level):
        return jnp.logical_and(has_next, bit_of(z + 1, level))

    def send_on(level, p, value):
        pay[level, :, p * step : (p + 1) * step] = value.astype(BF16)
        z_copy(level, p).start()

    def give_run(level, p):
        if level < cross:

            @pl.when(jnp.logical_and(gives(level), jnp.logical_not(takes(level))))
            def _():
                send_on(level, p, state[:, own_piece(p)])

    def handle(level, p):
        @pl.when(takes(level))
        def _():
            cols = own_piece(p)
            z_copy(level, p).wait_recv()
            forward(level, p).start()
            moved = carried[level, :, cols].astype(F32) * gone_in[2:3, cols]

            @pl.when(gives(level))
            def _():
                send_on(level, p, moved)

            state[:, cols] += moved
            give_run(level + 1, p)

    for p in range(pieces):
        cols = own_piece(p)
        s_copy(p).wait_recv()
        mine_s = state[:, cols]
        theirs_s = s_in[:, cols].astype(F32)
        state[:, cols] = jnp.where(first_core, mine_s, theirs_s) * gone_in[1:2, cols] + jnp.where(
            first_core, theirs_s, mine_s
        )
        give_run(1, p)
    for level in range(1, cross):

        @pl.when(jnp.logical_not(takes(level)))
        def _():
            carried[level] = jnp.zeros((STATES, width), BF16)

    for number, (start, mid, stop) in enumerate(joins):
        one, two = join_rows[number]
        runs[number] = run_of(start, mid) * fac[one : one + 1, :] + run_of(mid, stop) * fac[two : two + 1, :]
    for number in range(n // 2):
        local(order[number])
    for level in range(1, cross - 1):
        for p in range(pieces):
            handle(level, p)
    for number in range(n // 2, n):
        local(order[number])

    @pl.when(first_core)
    def _():
        carried[0] = jnp.zeros((STATES, width), BF16)

    @pl.when(jnp.logical_not(first_core))
    def _():
        rest.wait_recv()
        carried[0] = s_in[...]

    group = jnp.where(
        iota((step, step), 0) // HEAD_VALUES == iota((step, step), 1) // HEAD_VALUES, 1.0 / HEAD_VALUES, 0.0
    ).astype(BF16)
    last = cross - 1

    def finish(cols):
        shift = gone_in[3:4, cols]
        held = [carried[0, :, cols]]
        held += [(carried[level, :, cols].astype(F32) * shift).astype(BF16) for level in range(1, cross)]
        held = jnp.concatenate(held, axis=0)
        bands = [slice(r * 2 * CHUNK, (r + 1) * 2 * CHUNK) for r in range(rows_total // (2 * CHUNK))]
        for rows in bands:
            term = y[rows, cols] + dot(reads_all[rows, :], held) * ex[rows, cols]
            mean = dot((term * term).astype(BF16), group)
            out[rows, cols] = (
                hid[rows, cols].astype(F32) + term * lax.rsqrt(mean + 1e-05) * gain[:, cols]
            ).astype(BF16)

    @pl.when(gives(last))
    def _():
        for p in range(pieces):
            handle(last, p)

    for p in range(pieces):

        @pl.when(jnp.logical_not(gives(last)))
        def _():
            handle(last, p)

        finish(own_piece(p))
        for level in range(1, cross):

            @pl.when(takes(level))
            def _():
                forward(level, p).wait_recv()

        finish(other_piece(p))

    @pl.when(has_after)
    def _():
        for copy in halo:
            copy.wait_send()

    for bit in range(head_bits):
        for c in range(n):
            for kind in range(2):
                bc_copy(kind, bit, c).wait_send()
    for p in range(pieces):
        s_copy(p).wait_send()
        for level in range(1, cross):

            @pl.when(takes(level))
            def _():
                forward(level, p).wait_send()

            @pl.when(gives(level))
            def _():
                z_copy(level, p).wait_send()

    @pl.when(first_core)
    def _():
        rest.wait_send()


def body(
    residual_in,
    query_rows,
    key_rows,
    value_rows,
    bc_weight,
    decay_rate,
    level_codes,
    level_scale,
    positions,
    ssm_gain,
):
    rows, width = residual_in.shape
    n = rows // CHUNK
    ssm = decay_rate.shape[1]
    seq_size = lax.axis_size("seq")
    head_bits = lax.axis_size("head").bit_length() - 1
    cross = (seq_size * lax.axis_size("fsdp")).bit_length() - 1
    bits = max(head_bits, 1)
    joins, _, reads = plan(n)
    factors = 2 * n + 1 + 2 * len(joins) + len(reads)
    factors += -factors % 16
    half = width // 2
    pieces = half // PIECE if half % PIECE == 0 else 1
    levels = level_codes.shape[1]
    dma = pltpu.SemaphoreType.DMA
    any_spec = pl.BlockSpec(memory_space=pl.ANY)
    scratch = [
        pltpu.VMEM((rows, width), BF16),
        pltpu.VMEM((rows + CHUNK, width), BF16),
        pltpu.VMEM((rows + CHUNK, width), BF16),
        pltpu.VMEM((rows, width), BF16),
        pltpu.VMEM((2 * bc_weight.shape[0], bc_weight.shape[1]), BF16),
        pltpu.VMEM((ssm, rows), F32),
        pltpu.VMEM((levels, rows), jnp.int32),
        pltpu.VMEM((1, levels), F32),
        pltpu.VMEM((n, 1, CHUNK), jnp.int32),
        pltpu.VMEM((1, width), F32),
        pltpu.VMEM((rows, width), BF16),
        pltpu.VMEM((rows, width), BF16),
        pltpu.VMEM((2, bits, rows, STATES), BF16),
        pltpu.VMEM((2, bits, rows, STATES), BF16),
        pltpu.VMEM((rows, STATES), BF16),
        pltpu.VMEM((rows, cross * STATES), BF16),
        pltpu.VMEM((STATES, width), F32),
        pltpu.VMEM((n, STATES, width), F32),
        pltpu.VMEM((len(joins), STATES, width), F32),
        pltpu.VMEM((rows, width), F32),
        pltpu.VMEM((rows, width), F32),
        pltpu.VMEM((n, CHUNK, 4 * ssm), BF16),
        pltpu.VMEM((n, CHUNK, level_codes.shape[1]), F32),
        pltpu.VMEM((factors, width), F32),
        pltpu.VMEM((2 * ssm, width), BF16),
        pltpu.VMEM((8, width), F32),
        pltpu.VMEM((8, width), F32),
        pltpu.VMEM((STATES, width), BF16),
        pltpu.VMEM((STATES, width), BF16),
        pltpu.VMEM((cross, STATES, width), BF16),
        pltpu.VMEM((cross, STATES, width // 2), BF16),
        dma((5,)), dma((2, n)), dma((2, n)), dma, dma((2,)), dma((2,)), dma((2,)), dma((2,)),
        dma((2, bits, n)), dma((2, bits, n)), dma((pieces + 1,)), dma((pieces + 1,)),
        dma((cross, pieces)), dma((cross, pieces)), dma((cross, pieces)), dma((cross, pieces)),
    ]
    return pl.pallas_call(
        functools.partial(mixer_kernel, head_bits, cross, seq_size),
        in_specs=[any_spec] * 10,
        out_specs=pl.BlockSpec(memory_space=pltpu.VMEM),
        out_shape=pltpu.VMEM((rows, width), BF16),
        scratch_shapes=scratch,
        name="attend_and_mix",
        compiler_params=pltpu.CompilerParams(collective_id=0, has_side_effects=True, vmem_limit_bytes=56 * 2**20),
        cost_estimate=pl.CostEstimate(flops=rows * width * 8000, bytes_accessed=12 * rows * width, transcendentals=0),
    )(
        query_rows, key_rows, value_rows, residual_in, bc_weight, decay_rate.T, level_codes.T, level_scale[None, :],
        positions.reshape(n, 1, CHUNK), ssm_gain[None, :],
    )


def solution(mesh):
    in_specs = (
        P(("groups", "seq", "fsdp"), "head"),
        P(("groups", "seq", "fsdp"), "head"),
        P(("groups", "seq", "fsdp"), "head"),
        P(("groups", "seq", "fsdp"), "head"),
        P(("head", "fsdp"), None),
        P(("groups", "seq", "fsdp"), "head"),
        P(("groups", "seq", "fsdp"), None),
        P(),
        P(("groups", "seq", "fsdp")),
        P("head"),
    )
    out_specs = P(("groups", "seq", "fsdp"), "head")
    return jax.shard_map(body, mesh=mesh, in_specs=in_specs, out_specs=out_specs, check_vma=False)
```

```python
import functools
import math

import jax
import jax.numpy as jnp
from jax import lax
from jax.experimental import pallas as pl
from jax.experimental.pallas import tpu as pltpu
from jax.sharding import PartitionSpec as P

HEAD_DIM = 128
HEAD_VALUES = 64
STATES = 128
WINDOW = 128
CHUNK = 128
LOG2E = math.log2(math.e)
F32 = jnp.float32
BF16 = jnp.bfloat16
MESH = pl.DeviceIdType.MESH
PIECE = 128
UNIT = 256


def iota(shape, axis):
    return lax.broadcasted_iota(jnp.int32, shape, axis)


def dot(a, b):
    return jnp.dot(a, b, preferred_element_type=F32)


def dot_nt(a, b, precision=None):
    return lax.dot_general(a, b, (((1,), (1,)), ((), ())), precision=precision, preferred_element_type=F32)


def dot_tn(a, b):
    return lax.dot_general(a, b, (((0,), (0,)), ((), ())), preferred_element_type=F32)


def split2(x):
    hi = x.astype(BF16)
    lo = (x - hi.astype(F32)).astype(BF16)
    return jnp.concatenate([hi, lo], axis=1)


def plan(n):
    joins, reads = [], {}
    made = {}
    for i in range(n):
        for s in range(n.bit_length() - 1):
            if (i >> s) & 1:
                start = (i >> (s + 1)) << (s + 1)
                reads[i, s] = (start, start + (1 << s))
    def make(start, stop):
        if stop - start == 1 or (start, stop) in made:
            return
        mid = (start + stop) // 2
        make(start, mid)
        make(mid, stop)
        made[start, stop] = len(joins)
        joins.append((start, mid, stop))
    for i in range(n):
        for s in range(n.bit_length() - 1):
            if (i, s) in reads:
                make(*reads[i, s])
    return joins, made, reads


def mixer_kernel(
    head_bits, cross, seq_size,
    q_hbm, k_hbm, v_hbm, res_hbm, w_hbm, decay_hbm, codes_hbm, scale_hbm, pos_hbm, gain_hbm, out,
    q, k, v, res, w, decay, codes, scale, pos, gain, hid, fu, sent, came, b_all, reads_all, state, raw, runs, y, ex, ef,
    lam, fac, spread, gone, gone_in, gone_chip, gone_prev, s_bf, s_in, carried, pay,
    small_sem, in_sem, kv_sem, w_sem, halo_send, halo_recv, wx_sem, gone_sem, bc_send, bc_recv, s_send, s_recv,
    z_send, z_far, z_recv, f_send, f_recv, far_sem,
):
    rows_total, width = q.shape
    n = rows_total // CHUNK
    ssm = decay.shape[0]
    inner = n.bit_length() - 1
    low_levels = CHUNK.bit_length()
    first_level = rows_total.bit_length()
    half = width // 2
    head_pos = lax.axis_index("head")
    z = lax.axis_index("seq")
    f = lax.axis_index("fsdp")
    sibling = {"fsdp": 1 - f}
    ahead = {"seq": z + 1}
    after = {"seq": z + f, "fsdp": 1 - f}
    has_next = z + 1 < seq_size
    has_prev = z > 0
    has_after = jnp.logical_or(f == 0, has_next)
    has_before = jnp.logical_or(f == 1, has_prev)

    def head_partner(bit):
        up = lax.rem(head_pos // (1 << bit), 2)
        return {"head": head_pos + (1 << bit) * (1 - 2 * up)}

    def rows_of(c):
        if isinstance(c, int):
            return pl.ds(c * CHUNK, CHUNK)
        return pl.ds(pl.multiple_of(c * CHUNK, CHUNK), CHUNK)

    def next_rows(c):
        if isinstance(c, int):
            return pl.ds((c + 1) * CHUNK, CHUNK)
        return pl.ds(pl.multiple_of((c + 1) * CHUNK, CHUNK), CHUNK)

    def load_k(c):
        return pltpu.make_async_copy(k_hbm.at[rows_of(c)], k.at[next_rows(c)], kv_sem.at[0, c])

    def load_v(c):
        return pltpu.make_async_copy(v_hbm.at[rows_of(c)], v.at[next_rows(c)], kv_sem.at[1, c])

    def load_q(c):
        return pltpu.make_async_copy(q_hbm.at[rows_of(c)], q.at[rows_of(c)], in_sem.at[0, c])

    def load_res(c):
        return pltpu.make_async_copy(res_hbm.at[rows_of(c)], res.at[rows_of(c)], in_sem.at[1, c])

    def remote(src, dst, send, recv, device):
        return pltpu.make_async_remote_copy(src, dst, send, recv, device_id=device, device_id_type=MESH)

    barrier = pltpu.get_barrier_semaphore()

    def greet(device):
        pl.semaphore_signal(barrier, inc=1, device_id=device, device_id_type=MESH)

    for bit in range(head_bits):
        greet(head_partner(bit))
    greet(sibling)

    @pl.when(has_next)
    def _():
        greet(ahead)

    @pl.when(has_prev)
    def _():
        greet({"seq": z - 1})


    @pl.when(jnp.logical_and(f == 1, has_next))
    def _():
        greet(after)

    @pl.when(jnp.logical_and(f == 0, has_prev))
    def _():
        greet({"seq": z - 1, "fsdp": 1 - f})

    smalls = [
        pltpu.make_async_copy(src, dst, small_sem.at[number])
        for number, (src, dst) in enumerate(
            [(decay_hbm, decay), (codes_hbm, codes), (scale_hbm, scale), (pos_hbm, pos), (gain_hbm, gain)]
        )
    ]
    for copy in smalls:
        copy.start()
    depth = w_hbm.shape[0]
    own_rows = pl.ds(pl.multiple_of(f * depth, depth), depth)
    w_load = pltpu.make_async_copy(w_hbm, w.at[own_rows], w_sem)
    w_load.start()
    load_k(0).start()
    load_v(0).start()
    order = [(i + 1) % n for i in range(n)]
    links = head_bits + 1
    links += has_next.astype(jnp.int32) + has_prev.astype(jnp.int32)
    links += jnp.logical_and(f == 1, has_next).astype(jnp.int32) + jnp.logical_and(f == 0, has_prev).astype(jnp.int32)
    pl.semaphore_wait(barrier, links)
    @pl.when(jnp.logical_and(has_prev, has_next))
    def _():
        pl.semaphore_signal(far_sem, inc=1, device_id={"seq": z - 1}, device_id_type=MESH)

    tail = pl.ds(rows_total - WINDOW, WINDOW)
    halo = [
        remote(k_hbm.at[tail], k.at[pl.ds(0, WINDOW)], halo_send.at[0], halo_recv.at[0], after),
        remote(v_hbm.at[tail], v.at[pl.ds(0, WINDOW)], halo_send.at[1], halo_recv.at[1], after),
    ]

    @pl.when(has_after)
    def _():
        for copy in halo:
            copy.start()

    w_send = remote(w_hbm, w.at[own_rows], wx_sem.at[0], wx_sem.at[1], sibling)
    w_send.start()
    for c in order:
        if c:
            load_k(c).start()
            load_v(c).start()
        load_q(c).start()
        load_res(c).start()

    @pl.when(jnp.logical_not(has_before))
    def _():
        k[:CHUNK, :] = jnp.zeros((CHUNK, width), BF16)
        v[:CHUNK, :] = jnp.zeros((CHUNK, width), BF16)

    for copy in smalls:
        copy.wait()

    tri = jnp.where(iota((CHUNK, CHUNK), 1) <= iota((CHUNK, CHUNK), 0), 1.0, 0.0)
    decays = decay[...] * LOG2E
    stacked = jnp.concatenate([decays[:, c * CHUNK : (c + 1) * CHUNK] for c in range(n)], axis=0)
    sums = dot_nt(tri, stacked, lax.Precision.HIGHEST)
    total = sums[CHUNK - 1 :, :]
    rise = split2(jnp.exp2(0.5 * total - sums))
    fall = split2(jnp.exp2(sums - 0.5 * total))
    for c in range(n):
        parts = [side[:, a * n * ssm + c * ssm : a * n * ssm + (c + 1) * ssm] for side in (rise, fall) for a in range(2)]
        ef[c] = jnp.concatenate(parts, axis=1)
    tot = [total[:, c * ssm : (c + 1) * ssm] for c in range(n)]
    joins, made, reads = plan(n)

    def between(start, stop):
        return functools.reduce(lambda a, b: a + b, tot[start:stop], jnp.zeros_like(tot[0]))

    table = []

    def put(exponent):
        table.append(exponent)
        return len(table) - 1

    for c in range(n):
        put(0.5 * tot[c] + between(c + 1, n))
    for c in range(n):
        put(0.5 * tot[c] + between(0, c))
    all_row = put(between(0, n))

    def own_half(start, stop):
        return 0.5 * tot[start] if stop - start == 1 else jnp.zeros_like(tot[0])

    join_rows = [
        (put(own_half(start, mid) + between(mid, stop)), put(own_half(mid, stop))) for start, mid, stop in joins
    ]
    read_rows = {
        (i, s): put(own_half(*reads[i, s]) + between(reads[i, s][1], i) + 0.5 * tot[i]) for (i, s) in sorted(reads)
    }
    while len(table) % 16:
        put(jnp.zeros_like(tot[0]))
    same = lax.rem(iota((2 * ssm, width), 0), ssm) == iota((2 * ssm, width), 1) // HEAD_VALUES
    spread[...] = jnp.where(same, 1.0, 0.0).astype(BF16)
    fac[...] = dot(split2(jnp.exp2(-jnp.concatenate(table, axis=0))), spread[...])
    gone[...] = jnp.broadcast_to(fac[all_row : all_row + 1, :], gone.shape)
    eye = jnp.where(iota((CHUNK, CHUNK), 1) == iota((CHUNK, CHUNK), 0), 1.0, 0.0).astype(BF16)
    for c in range(n):
        code = codes[:, c * CHUNK : (c + 1) * CHUNK].astype(F32).astype(BF16)
        lam[c] = dot_nt(eye, code) * scale[...]

    gone_send = remote(gone, gone_in, gone_sem.at[0], gone_sem.at[1], sibling)
    gone_send.start()

    def bc_copy(kind, bit, c):
        return remote(
            sent.at[kind, bit, rows_of(c)], came.at[kind, bit, rows_of(c)], bc_send.at[kind, bit, c],
            bc_recv.at[kind, bit, c], head_partner(bit),
        )

    def summed(kind, c):
        rows = rows_of(c)
        value = sent[kind, 0, rows, :]
        for bit in range(head_bits):
            bc_copy(kind, bit, c).wait_recv()
            value = (sent[kind, bit, rows, :].astype(F32) + came[kind, bit, rows, :].astype(F32)).astype(BF16)
            if bit < head_bits - 1:
                sent[kind, bit + 1, rows, :] = value
                bc_copy(kind, bit + 1, c).start()
        return value

    def collect(c):
        rows = rows_of(c)
        b = summed(0, c)
        b_all[rows, :] = b
        chunk = dot_tn(b, fu[rows, :])
        raw[c] = chunk
        state[...] += chunk * fac[pl.ds(c, 1), :]

    state[...] = jnp.zeros_like(state)

    load_k(0).wait()
    load_v(0).wait()
    w_load.wait()
    w_send.wait()
    near = (iota((CHUNK, CHUNK), 0) - iota((CHUNK, CHUNK), 1)).astype(F32)
    far = near + float(WINDOW)
    factor = LOG2E / math.sqrt(HEAD_DIM)

    def attend(i, carry):
        c = lax.rem(i + 1, n)

        @pl.when(i < n - 1)
        def _():
            load_k(c).wait()
            load_v(c).wait()

        @pl.when(jnp.logical_and(i == n - 1, has_before))
        def _():
            for copy in halo:
                copy.wait_recv()

        load_q(c).wait()
        load_res(c).wait()
        rows = rows_of(c)
        both = pl.ds(pl.multiple_of(c * CHUNK, CHUNK), 2 * CHUNK)
        pos_col = jnp.broadcast_to(pos[c].astype(F32), (CHUNK, CHUNK)).T
        mask_cur = jnp.where((near >= 0) & (near <= pos_col), 0.0, -jnp.inf)
        mask_prev = jnp.where((far < float(WINDOW)) & (far <= pos_col), 0.0, -jnp.inf)
        mask = jnp.concatenate([mask_prev, mask_cur], axis=1)
        heads = [slice(h * HEAD_DIM, (h + 1) * HEAD_DIM) for h in range(width // HEAD_DIM)]
        scores = [dot_nt(q[rows, cols], k[both, cols]) + mask for cols in heads]
        tops = [jnp.max(s, axis=1, keepdims=True) for s in scores]
        raised = [jnp.exp2((s - top) * factor) for s, top in zip(scores, tops)]
        totals = [jnp.sum(e, axis=1, keepdims=True) for e in raised]
        weighted = [dot(e.astype(BF16), v[both, cols]) for e, cols in zip(raised, heads)]
        hidden = jnp.concatenate(
            [
                (res[rows, cols].astype(F32) + a * (1.0 / t)).astype(BF16)
                for cols, a, t in zip(heads, weighted, totals)
            ],
            axis=1,
        )
        hid[rows, :] = hidden

        part = dot(hidden, w[...]).astype(BF16)
        sent[0, 0, rows, :] = part[:, :STATES]
        sent[1, 0, rows, :] = part[:, STATES:]
        if head_bits:
            bc_copy(0, 0, c).start()
        fu[rows, :] = (dot(ef[c][:, 2 * ssm :], spread[...]) * hidden.astype(F32)).astype(BF16)
        return carry

    lax.fori_loop(0, n, attend, 0)
    gone_send.wait()
    first_core = f == 0
    mine = gone[0:1, :]
    theirs = gone_in[0:1, :]
    gone_chip[...] = jnp.broadcast_to(mine * theirs, gone_chip.shape)
    gone_in[1:2, :] = jnp.where(first_core, theirs, mine)
    gone_in[2:3, :] = mine * theirs
    gone_in[3:4, :] = jnp.where(first_core, 1.0, theirs)
    chip_send = remote(gone_chip, gone_prev, gone_sem.at[2], gone_sem.at[3], ahead)

    @pl.when(has_next)
    def _():
        chip_send.start()

    if head_bits:
        for number in range(n):
            bc_copy(1, 0, order[number]).start()
    for number in range(n):
        collect(order[number])

    pieces = half // PIECE if half % PIECE == 0 else 1
    step = half // pieces

    def own_piece(p):
        return pl.ds(pl.multiple_of(f * half + p * step, step), step)

    def other_piece(p):
        return pl.ds(pl.multiple_of((1 - f) * half + p * step, step), step)

    def s_copy(p):
        cols = other_piece(p)
        return remote(s_bf.at[:, cols], s_in.at[:, cols], s_send.at[p], s_recv.at[p], sibling)

    own_cols = pl.ds(pl.multiple_of(f * half, half), half)
    rest = remote(s_bf.at[:, own_cols], s_in.at[:, own_cols], s_send.at[pieces], s_recv.at[pieces], sibling)
    for p in range(pieces):
        s_bf[:, other_piece(p)] = state[:, other_piece(p)].astype(BF16)
        s_copy(p).start()
    s_bf[:, own_cols] = state[:, own_cols].astype(BF16)

    @pl.when(first_core)
    def _():
        rest.start()

    side = (CHUNK, CHUNK)
    differ = iota(side, 0) ^ iota(side, 1)
    causal = iota(side, 1) <= iota(side, 0)

    def run_of(start, stop):
        return raw[start] if stop - start == 1 else runs[made[start, stop]]

    def local(i):
        rows = rows_of(i)
        lam_c = lam[i]
        weight = jnp.broadcast_to(lam_c[:, 0:1], side)
        for level in range(1, low_levels):
            weight = jnp.where(differ >= 1 << level - 1, lam_c[:, level : level + 1], weight)
        b, c = b_all[rows, :], summed(1, i)
        shared = jnp.where(causal, dot_nt(c, b) * weight, 0.0)
        left = [shared.astype(BF16)]
        right = [fu[rows, :]]
        c32 = c.astype(F32)
        for s in range(inner):
            if (i, s) in reads:
                row = read_rows[i, s]
                left.append((c32 * lam_c[:, low_levels + s : low_levels + s + 1]).astype(BF16))
                right.append((run_of(*reads[i, s]) * fac[row : row + 1, :]).astype(BF16))
        for s in range(cross):
            reads_all[rows, s * STATES : (s + 1) * STATES] = (
                c32 * lam_c[:, first_level + s : first_level + s + 1]
            ).astype(BF16)
        terms = dot(jnp.concatenate(left, axis=1), jnp.concatenate(right, axis=0))
        grow = dot(ef[i][:, : 2 * ssm], spread[...])
        y[rows, :] = terms * grow
        ex[rows, :] = grow * fac[n + i : n + i + 1, :]

    def z_copy(level, p):
        return remote(
            pay.at[level, :, pl.ds(p * step, step)], carried.at[level, :, own_piece(p)], z_send.at[level, p],
            z_recv.at[level, p], ahead,
        )

    def far_copy(level, p):
        return remote(
            pay.at[level, :, pl.ds(p * step, step)], carried.at[level, :, own_piece(p)], z_far.at[level, p],
            z_recv.at[level, p], {"seq": z + 2},
        )

    def forward(level, p):
        cols = own_piece(p)
        return remote(
            carried.at[level, :, cols], carried.at[level, :, cols], f_send.at[level, p], f_recv.at[level, p], sibling
        )

    def bit_of(x, level):
        return lax.rem(x // (1 << level - 1), 2) == 1

    def takes(level):
        return bit_of(z, level)

    def gives(level):
        return jnp.logical_and(has_next, bit_of(z + 1, level))

    def direct(level, p):
        return level > 1 and p >= (pieces + 1) // 2

    def place(level):
        return lax.rem(z, 1 << level - 1)

    def sends_near(level, p):
        if direct(level, p):
            return jnp.logical_and(gives(level), jnp.logical_or(jnp.logical_not(takes(level)), place(level) > 0))
        return gives(level)

    def sends_far(level):
        return jnp.logical_and(gives(level), jnp.logical_not(takes(level)))

    def give_run(level, p):
        if level < cross:

            @pl.when(sends_far(level))
            def _():
                pay[level, :, p * step : (p + 1) * step] = state[:, own_piece(p)].astype(BF16)
                if direct(level, p):
                    far_copy(level, p).start()
                z_copy(level, p).start()

    def handle(level, p):
        @pl.when(takes(level))
        def _():
            cols = own_piece(p)
            z_copy(level, p).wait_recv()
            if direct(level, p):

                @pl.when(place(level) == 1)
                def _():
                    carried[level, :, cols] = (carried[level, :, cols].astype(F32) * gone_prev[0:1, cols]).astype(BF16)

            forward(level, p).start()
            moved = carried[level, :, cols].astype(F32) * gone_in[2:3, cols]

            @pl.when(sends_near(level, p))
            def _():
                pay[level, :, p * step : (p + 1) * step] = moved.astype(BF16)
                z_copy(level, p).start()

            state[:, cols] += moved
            give_run(level + 1, p)

    @pl.when(has_prev)
    def _():
        chip_send.wait_recv()

    @pl.when(z + 2 < seq_size)
    def _():
        pl.semaphore_wait(far_sem, 1)

    for p in range(pieces):
        cols = own_piece(p)
        s_copy(p).wait_recv()
        mine_s = state[:, cols]
        theirs_s = s_in[:, cols].astype(F32)
        state[:, cols] = jnp.where(first_core, mine_s, theirs_s) * gone_in[1:2, cols] + jnp.where(
            first_core, theirs_s, mine_s
        )
        give_run(1, p)
    for level in range(1, cross):

        @pl.when(jnp.logical_not(takes(level)))
        def _():
            carried[level] = jnp.zeros((STATES, width), BF16)

    for number, (start, mid, stop) in enumerate(joins):
        one, two = join_rows[number]
        runs[number] = run_of(start, mid) * fac[one : one + 1, :] + run_of(mid, stop) * fac[two : two + 1, :]
    for number in range(n // 2):
        local(order[number])
    for level in range(1, cross - 1):
        for p in range(pieces):
            handle(level, p)
    for number in range(n // 2, n):
        local(order[number])

    @pl.when(first_core)
    def _():
        carried[0] = jnp.zeros((STATES, width), BF16)

    @pl.when(jnp.logical_not(first_core))
    def _():
        rest.wait_recv()
        carried[0] = s_in[...]

    per_unit = UNIT // step if half % UNIT == 0 else 1
    unit = per_unit * step
    side = (unit, unit)
    group = jnp.where(
        iota(side, 0) // HEAD_VALUES == iota(side, 1) // HEAD_VALUES, 1.0 / HEAD_VALUES, 0.0
    ).astype(BF16)
    last = cross - 1

    def finish(cols):
        shift = gone_in[3:4, cols]
        held = [carried[0, :, cols]]
        held += [(carried[level, :, cols].astype(F32) * shift).astype(BF16) for level in range(1, cross)]
        held = jnp.concatenate(held, axis=0)
        bands = [slice(r * 2 * CHUNK, (r + 1) * 2 * CHUNK) for r in range(rows_total // (2 * CHUNK))]
        terms = [y[rows, cols] + dot(reads_all[rows, :], held) * ex[rows, cols] for rows in bands]
        means = [dot((term * term).astype(BF16), group) for term in terms]
        for rows, term, mean in zip(bands, terms, means):
            out[rows, cols] = (
                hid[rows, cols].astype(F32) + term * lax.rsqrt(mean + 1e-05) * gain[:, cols]
            ).astype(BF16)

    units = half // unit
    turned = jnp.logical_and(takes(last), place(last) > 0)

    @pl.when(gives(last))
    def _():
        for p in range(pieces):
            if not direct(last, p):
                handle(last, p)

    def handle_unit(number):
        for p in range(number * per_unit, (number + 1) * per_unit):
            if direct(last, p):
                handle(last, p)
            else:

                @pl.when(jnp.logical_not(gives(last)))
                def _():
                    handle(last, p)

    def wait_unit(number):
        for level in range(1, cross):

            @pl.when(takes(level))
            def _():
                for p in range(number * per_unit, (number + 1) * per_unit):
                    forward(level, p).wait_recv()

    def in_turn(turn, act):
        if units == 1:
            act(turn)
            return

        @pl.when(jnp.logical_not(turned))
        def _():
            act(turn)

        @pl.when(turned)
        def _():
            act(units - 1 - turn)

    for turn in range(units):
        in_turn(turn, handle_unit)
        number = jnp.where(turned, units - 1 - turn, turn)
        finish(pl.ds(pl.multiple_of(f * half + number * unit, unit), unit))
        in_turn(turn, wait_unit)
        finish(pl.ds(pl.multiple_of((1 - f) * half + number * unit, unit), unit))

    @pl.when(has_after)
    def _():
        for copy in halo:
            copy.wait_send()

    for bit in range(head_bits):
        for c in range(n):
            for kind in range(2):
                bc_copy(kind, bit, c).wait_send()
    for p in range(pieces):
        s_copy(p).wait_send()
        for level in range(1, cross):

            @pl.when(takes(level))
            def _():
                forward(level, p).wait_send()

            @pl.when(sends_near(level, p))
            def _():
                z_copy(level, p).wait_send()

            if direct(level, p):

                @pl.when(sends_far(level))
                def _():
                    far_copy(level, p).wait_send()

    @pl.when(has_next)
    def _():
        chip_send.wait_send()

    @pl.when(first_core)
    def _():
        rest.wait_send()


def body(
    residual_in,
    query_rows,
    key_rows,
    value_rows,
    bc_weight,
    decay_rate,
    level_codes,
    level_scale,
    positions,
    ssm_gain,
):
    rows, width = residual_in.shape
    n = rows // CHUNK
    ssm = decay_rate.shape[1]
    seq_size = lax.axis_size("seq")
    head_bits = lax.axis_size("head").bit_length() - 1
    cross = (seq_size * lax.axis_size("fsdp")).bit_length() - 1
    bits = max(head_bits, 1)
    joins, _, reads = plan(n)
    factors = 2 * n + 1 + 2 * len(joins) + len(reads)
    factors += -factors % 16
    half = width // 2
    pieces = half // PIECE if half % PIECE == 0 else 1
    levels = level_codes.shape[1]
    dma = pltpu.SemaphoreType.DMA
    any_spec = pl.BlockSpec(memory_space=pl.ANY)
    scratch = [
        pltpu.VMEM((rows, width), BF16),
        pltpu.VMEM((rows + CHUNK, width), BF16),
        pltpu.VMEM((rows + CHUNK, width), BF16),
        pltpu.VMEM((rows, width), BF16),
        pltpu.VMEM((2 * bc_weight.shape[0], bc_weight.shape[1]), BF16),
        pltpu.VMEM((ssm, rows), F32),
        pltpu.VMEM((levels, rows), jnp.int32),
        pltpu.VMEM((1, levels), F32),
        pltpu.VMEM((n, 1, CHUNK), jnp.int32),
        pltpu.VMEM((1, width), F32),
        pltpu.VMEM((rows, width), BF16),
        pltpu.VMEM((rows, width), BF16),
        pltpu.VMEM((2, bits, rows, STATES), BF16),
        pltpu.VMEM((2, bits, rows, STATES), BF16),
        pltpu.VMEM((rows, STATES), BF16),
        pltpu.VMEM((rows, cross * STATES), BF16),
        pltpu.VMEM((STATES, width), F32),
        pltpu.VMEM((n, STATES, width), F32),
        pltpu.VMEM((len(joins), STATES, width), F32),
        pltpu.VMEM((rows, width), F32),
        pltpu.VMEM((rows, width), F32),
        pltpu.VMEM((n, CHUNK, 4 * ssm), BF16),
        pltpu.VMEM((n, CHUNK, level_codes.shape[1]), F32),
        pltpu.VMEM((factors, width), F32),
        pltpu.VMEM((2 * ssm, width), BF16),
        pltpu.VMEM((8, width), F32),
        pltpu.VMEM((8, width), F32),
        pltpu.VMEM((8, width), F32),
        pltpu.VMEM((8, width), F32),
        pltpu.VMEM((STATES, width), BF16),
        pltpu.VMEM((STATES, width), BF16),
        pltpu.VMEM((cross, STATES, width), BF16),
        pltpu.VMEM((cross, STATES, width // 2), BF16),
        dma((5,)), dma((2, n)), dma((2, n)), dma, dma((2,)), dma((2,)), dma((2,)), dma((4,)),
        dma((2, bits, n)), dma((2, bits, n)), dma((pieces + 1,)), dma((pieces + 1,)),
        dma((cross, pieces)), dma((cross, pieces)), dma((cross, pieces)), dma((cross, pieces)), dma((cross, pieces)),
        pltpu.SemaphoreType.REGULAR,
    ]
    return pl.pallas_call(
        functools.partial(mixer_kernel, head_bits, cross, seq_size),
        in_specs=[any_spec] * 10,
        out_specs=pl.BlockSpec(memory_space=pltpu.VMEM),
        out_shape=pltpu.VMEM((rows, width), BF16),
        scratch_shapes=scratch,
        name="attend_and_mix",
        compiler_params=pltpu.CompilerParams(collective_id=0, has_side_effects=True, vmem_limit_bytes=56 * 2**20),
        cost_estimate=pl.CostEstimate(flops=rows * width * 8000, bytes_accessed=12 * rows * width, transcendentals=0),
    )(
        query_rows, key_rows, value_rows, residual_in, bc_weight, decay_rate.T, level_codes.T, level_scale[None, :],
        positions.reshape(n, 1, CHUNK), ssm_gain[None, :],
    )


def solution(mesh):
    in_specs = (
        P(("groups", "seq", "fsdp"), "head"),
        P(("groups", "seq", "fsdp"), "head"),
        P(("groups", "seq", "fsdp"), "head"),
        P(("groups", "seq", "fsdp"), "head"),
        P(("head", "fsdp"), None),
        P(("groups", "seq", "fsdp"), "head"),
        P(("groups", "seq", "fsdp"), None),
        P(),
        P(("groups", "seq", "fsdp")),
        P("head"),
    )
    out_specs = P(("groups", "seq", "fsdp"), "head")
    return jax.shard_map(body, mesh=mesh, in_specs=in_specs, out_specs=out_specs, check_vma=False)
```

```python
import functools
import math

import jax
import jax.numpy as jnp
from jax import lax
from jax.experimental import pallas as pl
from jax.experimental.pallas import tpu as pltpu
from jax.sharding import PartitionSpec as P

HEAD_DIM = 128
HEAD_VALUES = 64
STATES = 128
WINDOW = 128
CHUNK = 128
LOG2E = math.log2(math.e)
F32 = jnp.float32
BF16 = jnp.bfloat16
MESH = pl.DeviceIdType.MESH
PIECE = 128
UNIT = 256


def iota(shape, axis):
    return lax.broadcasted_iota(jnp.int32, shape, axis)


def dot(a, b):
    return jnp.dot(a, b, preferred_element_type=F32)


def dot_nt(a, b, precision=None):
    return lax.dot_general(a, b, (((1,), (1,)), ((), ())), precision=precision, preferred_element_type=F32)


def dot_tn(a, b):
    return lax.dot_general(a, b, (((0,), (0,)), ((), ())), preferred_element_type=F32)


def split2(x):
    hi = x.astype(BF16)
    lo = (x - hi.astype(F32)).astype(BF16)
    return jnp.concatenate([hi, lo], axis=1)


def plan(n):
    joins, reads = [], {}
    made = {}
    for i in range(n):
        for s in range(n.bit_length() - 1):
            if (i >> s) & 1:
                start = (i >> (s + 1)) << (s + 1)
                reads[i, s] = (start, start + (1 << s))
    def make(start, stop):
        if stop - start == 1 or (start, stop) in made:
            return
        mid = (start + stop) // 2
        make(start, mid)
        make(mid, stop)
        made[start, stop] = len(joins)
        joins.append((start, mid, stop))
    for i in range(n):
        for s in range(n.bit_length() - 1):
            if (i, s) in reads:
                make(*reads[i, s])
    return joins, made, reads


def mixer_kernel(
    head_bits, cross, seq_size,
    q_hbm, k_hbm, v_hbm, res_hbm, w_hbm, decay_hbm, codes_hbm, scale_hbm, pos_hbm, gain_hbm, out,
    q, k, v, res, w, decay, codes, scale, pos, gain, hid, fu, sent, came, b_all, reads_all, state, raw, runs, y, ex, ef,
    lam, fac, spread, gone, gone_in, gone_chip, gone_prev, s_bf, s_in, carried, pay,
    small_sem, in_sem, kv_sem, w_sem, halo_send, halo_recv, wx_sem, gone_sem, bc_send, bc_recv, s_send, s_recv,
    z_send, z_far, z_recv, f_send, f_recv, far_sem,
):
    rows_total, width = q.shape
    n = rows_total // CHUNK
    ssm = decay.shape[0]
    inner = n.bit_length() - 1
    low_levels = CHUNK.bit_length()
    first_level = rows_total.bit_length()
    half = width // 2
    head_pos = lax.axis_index("head")
    z = lax.axis_index("seq")
    f = lax.axis_index("fsdp")
    sibling = {"fsdp": 1 - f}
    ahead = {"seq": z + 1}
    after = {"seq": z + f, "fsdp": 1 - f}
    has_next = z + 1 < seq_size
    has_prev = z > 0
    has_after = jnp.logical_or(f == 0, has_next)
    has_before = jnp.logical_or(f == 1, has_prev)

    def head_partner(bit):
        up = lax.rem(head_pos // (1 << bit), 2)
        return {"head": head_pos + (1 << bit) * (1 - 2 * up)}

    def rows_of(c):
        if isinstance(c, int):
            return pl.ds(c * CHUNK, CHUNK)
        return pl.ds(pl.multiple_of(c * CHUNK, CHUNK), CHUNK)

    def next_rows(c):
        if isinstance(c, int):
            return pl.ds((c + 1) * CHUNK, CHUNK)
        return pl.ds(pl.multiple_of((c + 1) * CHUNK, CHUNK), CHUNK)

    def load_k(c):
        return pltpu.make_async_copy(k_hbm.at[rows_of(c)], k.at[next_rows(c)], kv_sem.at[0, c])

    def load_v(c):
        return pltpu.make_async_copy(v_hbm.at[rows_of(c)], v.at[next_rows(c)], kv_sem.at[1, c])

    def load_q(c):
        return pltpu.make_async_copy(q_hbm.at[rows_of(c)], q.at[rows_of(c)], in_sem.at[0, c])

    def load_res(c):
        return pltpu.make_async_copy(res_hbm.at[rows_of(c)], res.at[rows_of(c)], in_sem.at[1, c])

    def remote(src, dst, send, recv, device):
        return pltpu.make_async_remote_copy(src, dst, send, recv, device_id=device, device_id_type=MESH)

    barrier = pltpu.get_barrier_semaphore()

    def greet(device):
        pl.semaphore_signal(barrier, inc=1, device_id=device, device_id_type=MESH)

    for bit in range(head_bits):
        greet(head_partner(bit))
    greet(sibling)

    @pl.when(has_next)
    def _():
        greet(ahead)

    @pl.when(has_prev)
    def _():
        greet({"seq": z - 1})


    @pl.when(jnp.logical_and(f == 1, has_next))
    def _():
        greet(after)

    @pl.when(jnp.logical_and(f == 0, has_prev))
    def _():
        greet({"seq": z - 1, "fsdp": 1 - f})

    smalls = [
        pltpu.make_async_copy(src, dst, small_sem.at[number])
        for number, (src, dst) in enumerate(
            [(decay_hbm, decay), (codes_hbm, codes), (scale_hbm, scale), (pos_hbm, pos), (gain_hbm, gain)]
        )
    ]
    for copy in smalls:
        copy.start()
    depth = w_hbm.shape[0]
    own_rows = pl.ds(pl.multiple_of(f * depth, depth), depth)
    w_load = pltpu.make_async_copy(w_hbm, w.at[own_rows], w_sem)
    w_load.start()
    load_k(0).start()
    load_v(0).start()
    order = [(i + 1) % n for i in range(n)]
    links = head_bits + 1
    links += has_next.astype(jnp.int32) + has_prev.astype(jnp.int32)
    links += jnp.logical_and(f == 1, has_next).astype(jnp.int32) + jnp.logical_and(f == 0, has_prev).astype(jnp.int32)
    pl.semaphore_wait(barrier, links)
    @pl.when(jnp.logical_and(has_prev, has_next))
    def _():
        pl.semaphore_signal(far_sem, inc=1, device_id={"seq": z - 1}, device_id_type=MESH)

    tail = pl.ds(rows_total - WINDOW, WINDOW)
    halo = [
        remote(k_hbm.at[tail], k.at[pl.ds(0, WINDOW)], halo_send.at[0], halo_recv.at[0], after),
        remote(v_hbm.at[tail], v.at[pl.ds(0, WINDOW)], halo_send.at[1], halo_recv.at[1], after),
    ]

    @pl.when(has_after)
    def _():
        for copy in halo:
            copy.start()

    w_send = remote(w_hbm, w.at[own_rows], wx_sem.at[0], wx_sem.at[1], sibling)
    w_send.start()
    for c in order:
        if c:
            load_k(c).start()
            load_v(c).start()
        load_q(c).start()
        load_res(c).start()

    @pl.when(jnp.logical_not(has_before))
    def _():
        k[:CHUNK, :] = jnp.zeros((CHUNK, width), BF16)
        v[:CHUNK, :] = jnp.zeros((CHUNK, width), BF16)

    for copy in smalls:
        copy.wait()

    tri = jnp.where(iota((CHUNK, CHUNK), 1) <= iota((CHUNK, CHUNK), 0), 1.0, 0.0)
    decays = decay[...] * LOG2E
    stacked = jnp.concatenate([decays[:, c * CHUNK : (c + 1) * CHUNK] for c in range(n)], axis=0)
    sums = dot_nt(tri, stacked, lax.Precision.HIGHEST)
    total = sums[CHUNK - 1 :, :]
    rise = split2(jnp.exp2(0.5 * total - sums))
    fall = split2(jnp.exp2(sums - 0.5 * total))
    for c in range(n):
        parts = [side[:, a * n * ssm + c * ssm : a * n * ssm + (c + 1) * ssm] for side in (rise, fall) for a in range(2)]
        ef[c] = jnp.concatenate(parts, axis=1)
    tot = [total[:, c * ssm : (c + 1) * ssm] for c in range(n)]
    joins, made, reads = plan(n)

    def between(start, stop):
        return functools.reduce(lambda a, b: a + b, tot[start:stop], jnp.zeros_like(tot[0]))

    table = []

    def put(exponent):
        table.append(exponent)
        return len(table) - 1

    for c in range(n):
        put(0.5 * tot[c] + between(c + 1, n))
    for c in range(n):
        put(0.5 * tot[c] + between(0, c))
    all_row = put(between(0, n))

    def own_half(start, stop):
        return 0.5 * tot[start] if stop - start == 1 else jnp.zeros_like(tot[0])

    join_rows = [
        (put(own_half(start, mid) + between(mid, stop)), put(own_half(mid, stop))) for start, mid, stop in joins
    ]
    read_rows = {
        (i, s): put(own_half(*reads[i, s]) + between(reads[i, s][1], i) + 0.5 * tot[i]) for (i, s) in sorted(reads)
    }
    while len(table) % 16:
        put(jnp.zeros_like(tot[0]))
    same = lax.rem(iota((2 * ssm, width), 0), ssm) == iota((2 * ssm, width), 1) // HEAD_VALUES
    spread[...] = jnp.where(same, 1.0, 0.0).astype(BF16)
    fac[...] = dot(split2(jnp.exp2(-jnp.concatenate(table, axis=0))), spread[...])
    gone[...] = jnp.broadcast_to(fac[all_row : all_row + 1, :], gone.shape)
    eye = jnp.where(iota((CHUNK, CHUNK), 1) == iota((CHUNK, CHUNK), 0), 1.0, 0.0).astype(BF16)
    for c in range(n):
        code = codes[:, c * CHUNK : (c + 1) * CHUNK].astype(F32).astype(BF16)
        lam[c] = dot_nt(eye, code) * scale[...]

    gone_send = remote(gone, gone_in, gone_sem.at[0], gone_sem.at[1], sibling)
    gone_send.start()

    def bc_copy(kind, bit, c):
        return remote(
            sent.at[kind, bit, rows_of(c)], came.at[kind, bit, rows_of(c)], bc_send.at[kind, bit, c],
            bc_recv.at[kind, bit, c], head_partner(bit),
        )

    def summed(kind, c):
        rows = rows_of(c)
        value = sent[kind, 0, rows, :]
        for bit in range(head_bits):
            bc_copy(kind, bit, c).wait_recv()
            value = (sent[kind, bit, rows, :].astype(F32) + came[kind, bit, rows, :].astype(F32)).astype(BF16)
            if bit < head_bits - 1:
                sent[kind, bit + 1, rows, :] = value
                bc_copy(kind, bit + 1, c).start()
        return value

    def collect(c):
        rows = rows_of(c)
        b = summed(0, c)
        b_all[rows, :] = b
        chunk = dot_tn(b, fu[rows, :])
        raw[c] = chunk
        state[...] += chunk * fac[pl.ds(c, 1), :]

    state[...] = jnp.zeros_like(state)

    load_k(0).wait()
    load_v(0).wait()
    w_load.wait()
    w_send.wait()
    near = (iota((CHUNK, CHUNK), 0) - iota((CHUNK, CHUNK), 1)).astype(F32)
    far = near + float(WINDOW)
    factor = LOG2E / math.sqrt(HEAD_DIM)

    def attend(i, carry):
        c = lax.rem(i + 1, n)

        @pl.when(i < n - 1)
        def _():
            load_k(c).wait()
            load_v(c).wait()

        @pl.when(jnp.logical_and(i == n - 1, has_before))
        def _():
            for copy in halo:
                copy.wait_recv()

        load_q(c).wait()
        load_res(c).wait()
        rows = rows_of(c)
        both = pl.ds(pl.multiple_of(c * CHUNK, CHUNK), 2 * CHUNK)
        pos_col = jnp.broadcast_to(pos[c].astype(F32), (CHUNK, CHUNK)).T
        mask_cur = jnp.where((near >= 0) & (near <= pos_col), 0.0, -jnp.inf)
        mask_prev = jnp.where((far < float(WINDOW)) & (far <= pos_col), 0.0, -jnp.inf)
        mask = jnp.concatenate([mask_prev, mask_cur], axis=1)
        heads = [slice(h * HEAD_DIM, (h + 1) * HEAD_DIM) for h in range(width // HEAD_DIM)]
        scores = [dot_nt(q[rows, cols], k[both, cols]) + mask for cols in heads]
        tops = [jnp.max(s, axis=1, keepdims=True) for s in scores]
        raised = [jnp.exp2((s - top) * factor) for s, top in zip(scores, tops)]
        totals = [jnp.sum(e, axis=1, keepdims=True) for e in raised]
        weighted = [dot(e.astype(BF16), v[both, cols]) for e, cols in zip(raised, heads)]
        hidden = jnp.concatenate(
            [
                (res[rows, cols].astype(F32) + a * (1.0 / t)).astype(BF16)
                for cols, a, t in zip(heads, weighted, totals)
            ],
            axis=1,
        )
        hid[rows, :] = hidden

        part = dot(hidden, w[...]).astype(BF16)
        sent[0, 0, rows, :] = part[:, :STATES]
        sent[1, 0, rows, :] = part[:, STATES:]
        if head_bits:
            bc_copy(0, 0, c).start()
        fu[rows, :] = (dot(ef[c][:, 2 * ssm :], spread[...]) * hidden.astype(F32)).astype(BF16)
        return carry

    lax.fori_loop(0, n, attend, 0)
    gone_send.wait()
    first_core = f == 0
    mine = gone[0:1, :]
    theirs = gone_in[0:1, :]
    gone_chip[...] = jnp.broadcast_to(mine * theirs, gone_chip.shape)
    gone_in[1:2, :] = jnp.where(first_core, theirs, mine)
    gone_in[2:3, :] = mine * theirs
    gone_in[3:4, :] = jnp.where(first_core, 1.0, theirs)
    chip_send = remote(gone_chip, gone_prev, gone_sem.at[2], gone_sem.at[3], ahead)

    @pl.when(has_next)
    def _():
        chip_send.start()

    if head_bits:
        for number in range(n):
            bc_copy(1, 0, order[number]).start()
    for number in range(n):
        collect(order[number])

    pieces = half // PIECE if half % PIECE == 0 else 1
    step = half // pieces

    def own_piece(p):
        return pl.ds(pl.multiple_of(f * half + p * step, step), step)

    def other_piece(p):
        return pl.ds(pl.multiple_of((1 - f) * half + p * step, step), step)

    def s_copy(p):
        cols = other_piece(p)
        return remote(s_bf.at[:, cols], s_in.at[:, cols], s_send.at[p], s_recv.at[p], sibling)

    own_cols = pl.ds(pl.multiple_of(f * half, half), half)
    rest = remote(s_bf.at[:, own_cols], s_in.at[:, own_cols], s_send.at[pieces], s_recv.at[pieces], sibling)
    for p in range(pieces):
        s_bf[:, other_piece(p)] = state[:, other_piece(p)].astype(BF16)
        s_copy(p).start()
    s_bf[:, own_cols] = state[:, own_cols].astype(BF16)

    @pl.when(first_core)
    def _():
        rest.start()

    side = (CHUNK, CHUNK)
    differ = iota(side, 0) ^ iota(side, 1)
    causal = iota(side, 1) <= iota(side, 0)

    def run_of(start, stop):
        return raw[start] if stop - start == 1 else runs[made[start, stop]]

    def local(i):
        rows = rows_of(i)
        lam_c = lam[i]
        weight = jnp.broadcast_to(lam_c[:, 0:1], side)
        for level in range(1, low_levels):
            weight = jnp.where(differ >= 1 << level - 1, lam_c[:, level : level + 1], weight)
        b, c = b_all[rows, :], summed(1, i)
        shared = jnp.where(causal, dot_nt(c, b) * weight, 0.0)
        left = [shared.astype(BF16)]
        right = [fu[rows, :]]
        c32 = c.astype(F32)
        for s in range(inner):
            if (i, s) in reads:
                row = read_rows[i, s]
                left.append((c32 * lam_c[:, low_levels + s : low_levels + s + 1]).astype(BF16))
                right.append((run_of(*reads[i, s]) * fac[row : row + 1, :]).astype(BF16))
        for s in range(cross):
            reads_all[rows, s * STATES : (s + 1) * STATES] = (
                c32 * lam_c[:, first_level + s : first_level + s + 1]
            ).astype(BF16)
        terms = dot(jnp.concatenate(left, axis=1), jnp.concatenate(right, axis=0))
        grow = dot(ef[i][:, : 2 * ssm], spread[...])
        y[rows, :] = terms * grow
        ex[rows, :] = grow * fac[n + i : n + i + 1, :]

    def z_copy(level, p):
        return remote(
            pay.at[level, :, pl.ds(p * step, step)], carried.at[level, :, own_piece(p)], z_send.at[level, p],
            z_recv.at[level, p], ahead,
        )

    def far_copy(level, p):
        return remote(
            pay.at[level, :, pl.ds(p * step, step)], carried.at[level, :, own_piece(p)], z_far.at[level, p],
            z_recv.at[level, p], {"seq": z + 2},
        )

    def forward(level, p):
        cols = own_piece(p)
        return remote(
            carried.at[level, :, cols], carried.at[level, :, cols], f_send.at[level, p], f_recv.at[level, p], sibling
        )

    def bit_of(x, level):
        return lax.rem(x // (1 << level - 1), 2) == 1

    def takes(level):
        return bit_of(z, level)

    def gives(level):
        return jnp.logical_and(has_next, bit_of(z + 1, level))

    def direct(level, p):
        return level > 1 and p >= (pieces + 1) // 2

    def place(level):
        return lax.rem(z, 1 << level - 1)

    def sends_near(level, p):
        if direct(level, p):
            return jnp.logical_and(gives(level), jnp.logical_or(jnp.logical_not(takes(level)), place(level) > 0))
        return gives(level)

    def sends_far(level):
        return jnp.logical_and(gives(level), jnp.logical_not(takes(level)))

    def give_run(level, p):
        if level < cross:

            @pl.when(sends_far(level))
            def _():
                pay[level, :, p * step : (p + 1) * step] = state[:, own_piece(p)].astype(BF16)
                if direct(level, p):
                    far_copy(level, p).start()
                z_copy(level, p).start()

    def handle(level, p):
        @pl.when(takes(level))
        def _():
            cols = own_piece(p)
            z_copy(level, p).wait_recv()
            if direct(level, p):

                @pl.when(place(level) == 1)
                def _():
                    carried[level, :, cols] = (carried[level, :, cols].astype(F32) * gone_prev[0:1, cols]).astype(BF16)

            forward(level, p).start()
            moved = carried[level, :, cols].astype(F32) * gone_in[2:3, cols]

            @pl.when(sends_near(level, p))
            def _():
                pay[level, :, p * step : (p + 1) * step] = moved.astype(BF16)
                z_copy(level, p).start()

            state[:, cols] += moved
            give_run(level + 1, p)

    @pl.when(has_prev)
    def _():
        chip_send.wait_recv()

    @pl.when(z + 2 < seq_size)
    def _():
        pl.semaphore_wait(far_sem, 1)

    for p in range(pieces):
        cols = own_piece(p)
        s_copy(p).wait_recv()
        mine_s = state[:, cols]
        theirs_s = s_in[:, cols].astype(F32)
        state[:, cols] = jnp.where(first_core, mine_s, theirs_s) * gone_in[1:2, cols] + jnp.where(
            first_core, theirs_s, mine_s
        )
        give_run(1, p)
    for level in range(1, cross):

        @pl.when(jnp.logical_not(takes(level)))
        def _():
            carried[level] = jnp.zeros((STATES, width), BF16)

    for number, (start, mid, stop) in enumerate(joins):
        one, two = join_rows[number]
        runs[number] = run_of(start, mid) * fac[one : one + 1, :] + run_of(mid, stop) * fac[two : two + 1, :]
    for number in range(n // 4):
        local(order[number])
    for level in range(1, cross - 1):
        for p in range(pieces):
            handle(level, p)
    for number in range(n // 4, n):
        local(order[number])

    @pl.when(first_core)
    def _():
        carried[0] = jnp.zeros((STATES, width), BF16)

    @pl.when(jnp.logical_not(first_core))
    def _():
        rest.wait_recv()
        carried[0] = s_in[...]

    per_unit = UNIT // step if half % UNIT == 0 else 1
    unit = per_unit * step
    side = (unit, unit)
    group = jnp.where(
        iota(side, 0) // HEAD_VALUES == iota(side, 1) // HEAD_VALUES, 1.0 / HEAD_VALUES, 0.0
    ).astype(BF16)
    last = cross - 1

    def finish(cols):
        shift = gone_in[3:4, cols]
        held = [carried[0, :, cols]]
        held += [(carried[level, :, cols].astype(F32) * shift).astype(BF16) for level in range(1, cross)]
        held = jnp.concatenate(held, axis=0)
        bands = [slice(r * 2 * CHUNK, (r + 1) * 2 * CHUNK) for r in range(rows_total // (2 * CHUNK))]
        terms = [y[rows, cols] + dot(reads_all[rows, :], held) * ex[rows, cols] for rows in bands]
        means = [dot((term * term).astype(BF16), group) for term in terms]
        for rows, term, mean in zip(bands, terms, means):
            out[rows, cols] = (
                hid[rows, cols].astype(F32) + term * lax.rsqrt(mean + 1e-05) * gain[:, cols]
            ).astype(BF16)

    units = half // unit
    turned = jnp.logical_and(takes(last), place(last) > 0)

    @pl.when(gives(last))
    def _():
        for p in range(pieces):
            if not direct(last, p):
                handle(last, p)

    def handle_unit(number):
        for p in range(number * per_unit, (number + 1) * per_unit):
            if direct(last, p):
                handle(last, p)
            else:

                @pl.when(jnp.logical_not(gives(last)))
                def _():
                    handle(last, p)

    def wait_unit(number):
        for level in range(1, cross):

            @pl.when(takes(level))
            def _():
                for p in range(number * per_unit, (number + 1) * per_unit):
                    forward(level, p).wait_recv()

    def in_turn(turn, act):
        if units == 1:
            act(turn)
            return

        @pl.when(jnp.logical_not(turned))
        def _():
            act(turn)

        @pl.when(turned)
        def _():
            act(units - 1 - turn)

    for turn in range(units):
        in_turn(turn, handle_unit)
        number = jnp.where(turned, units - 1 - turn, turn)
        finish(pl.ds(pl.multiple_of(f * half + number * unit, unit), unit))
        in_turn(turn, wait_unit)
        finish(pl.ds(pl.multiple_of((1 - f) * half + number * unit, unit), unit))

    @pl.when(has_after)
    def _():
        for copy in halo:
            copy.wait_send()

    for bit in range(head_bits):
        for c in range(n):
            for kind in range(2):
                bc_copy(kind, bit, c).wait_send()
    for p in range(pieces):
        s_copy(p).wait_send()
        for level in range(1, cross):

            @pl.when(takes(level))
            def _():
                forward(level, p).wait_send()

            @pl.when(sends_near(level, p))
            def _():
                z_copy(level, p).wait_send()

            if direct(level, p):

                @pl.when(sends_far(level))
                def _():
                    far_copy(level, p).wait_send()

    @pl.when(has_next)
    def _():
        chip_send.wait_send()

    @pl.when(first_core)
    def _():
        rest.wait_send()


def body(
    residual_in,
    query_rows,
    key_rows,
    value_rows,
    bc_weight,
    decay_rate,
    level_codes,
    level_scale,
    positions,
    ssm_gain,
):
    rows, width = residual_in.shape
    n = rows // CHUNK
    ssm = decay_rate.shape[1]
    seq_size = lax.axis_size("seq")
    head_bits = lax.axis_size("head").bit_length() - 1
    cross = (seq_size * lax.axis_size("fsdp")).bit_length() - 1
    bits = max(head_bits, 1)
    joins, _, reads = plan(n)
    factors = 2 * n + 1 + 2 * len(joins) + len(reads)
    factors += -factors % 16
    half = width // 2
    pieces = half // PIECE if half % PIECE == 0 else 1
    levels = level_codes.shape[1]
    dma = pltpu.SemaphoreType.DMA
    any_spec = pl.BlockSpec(memory_space=pl.ANY)
    scratch = [
        pltpu.VMEM((rows, width), BF16),
        pltpu.VMEM((rows + CHUNK, width), BF16),
        pltpu.VMEM((rows + CHUNK, width), BF16),
        pltpu.VMEM((rows, width), BF16),
        pltpu.VMEM((2 * bc_weight.shape[0], bc_weight.shape[1]), BF16),
        pltpu.VMEM((ssm, rows), F32),
        pltpu.VMEM((levels, rows), jnp.int32),
        pltpu.VMEM((1, levels), F32),
        pltpu.VMEM((n, 1, CHUNK), jnp.int32),
        pltpu.VMEM((1, width), F32),
        pltpu.VMEM((rows, width), BF16),
        pltpu.VMEM((rows, width), BF16),
        pltpu.VMEM((2, bits, rows, STATES), BF16),
        pltpu.VMEM((2, bits, rows, STATES), BF16),
        pltpu.VMEM((rows, STATES), BF16),
        pltpu.VMEM((rows, cross * STATES), BF16),
        pltpu.VMEM((STATES, width), F32),
        pltpu.VMEM((n, STATES, width), F32),
        pltpu.VMEM((len(joins), STATES, width), F32),
        pltpu.VMEM((rows, width), F32),
        pltpu.VMEM((rows, width), F32),
        pltpu.VMEM((n, CHUNK, 4 * ssm), BF16),
        pltpu.VMEM((n, CHUNK, level_codes.shape[1]), F32),
        pltpu.VMEM((factors, width), F32),
        pltpu.VMEM((2 * ssm, width), BF16),
        pltpu.VMEM((8, width), F32),
        pltpu.VMEM((8, width), F32),
        pltpu.VMEM((8, width), F32),
        pltpu.VMEM((8, width), F32),
        pltpu.VMEM((STATES, width), BF16),
        pltpu.VMEM((STATES, width), BF16),
        pltpu.VMEM((cross, STATES, width), BF16),
        pltpu.VMEM((cross, STATES, width // 2), BF16),
        dma((5,)), dma((2, n)), dma((2, n)), dma, dma((2,)), dma((2,)), dma((2,)), dma((4,)),
        dma((2, bits, n)), dma((2, bits, n)), dma((pieces + 1,)), dma((pieces + 1,)),
        dma((cross, pieces)), dma((cross, pieces)), dma((cross, pieces)), dma((cross, pieces)), dma((cross, pieces)),
        pltpu.SemaphoreType.REGULAR,
    ]
    return pl.pallas_call(
        functools.partial(mixer_kernel, head_bits, cross, seq_size),
        in_specs=[any_spec] * 10,
        out_specs=pl.BlockSpec(memory_space=pltpu.VMEM),
        out_shape=pltpu.VMEM((rows, width), BF16),
        scratch_shapes=scratch,
        name="attend_and_mix",
        compiler_params=pltpu.CompilerParams(collective_id=0, has_side_effects=True, vmem_limit_bytes=56 * 2**20),
        cost_estimate=pl.CostEstimate(flops=rows * width * 8000, bytes_accessed=12 * rows * width, transcendentals=0),
    )(
        query_rows, key_rows, value_rows, residual_in, bc_weight, decay_rate.T, level_codes.T, level_scale[None, :],
        positions.reshape(n, 1, CHUNK), ssm_gain[None, :],
    )


def solution(mesh):
    in_specs = (
        P(("groups", "seq", "fsdp"), "head"),
        P(("groups", "seq", "fsdp"), "head"),
        P(("groups", "seq", "fsdp"), "head"),
        P(("groups", "seq", "fsdp"), "head"),
        P(("head", "fsdp"), None),
        P(("groups", "seq", "fsdp"), "head"),
        P(("groups", "seq", "fsdp"), None),
        P(),
        P(("groups", "seq", "fsdp")),
        P("head"),
    )
    out_specs = P(("groups", "seq", "fsdp"), "head")
    return jax.shard_map(body, mesh=mesh, in_specs=in_specs, out_specs=out_specs, check_vma=False)
```

```python
import functools
import math

import jax
import jax.numpy as jnp
from jax import lax
from jax.experimental import pallas as pl
from jax.experimental.pallas import tpu as pltpu
from jax.sharding import PartitionSpec as P

HEAD_DIM = 128
HEAD_VALUES = 64
STATES = 128
WINDOW = 128
CHUNK = 128
LOG2E = math.log2(math.e)
F32 = jnp.float32
BF16 = jnp.bfloat16
MESH = pl.DeviceIdType.MESH
PIECE = 256
UNIT = 256


def iota(shape, axis):
    return lax.broadcasted_iota(jnp.int32, shape, axis)


def dot(a, b):
    return jnp.dot(a, b, preferred_element_type=F32)


def dot_nt(a, b, precision=None):
    return lax.dot_general(a, b, (((1,), (1,)), ((), ())), precision=precision, preferred_element_type=F32)


def dot_tn(a, b):
    return lax.dot_general(a, b, (((0,), (0,)), ((), ())), preferred_element_type=F32)


def split2(x):
    hi = x.astype(BF16)
    lo = (x - hi.astype(F32)).astype(BF16)
    return jnp.concatenate([hi, lo], axis=1)


def plan(n):
    joins, reads = [], {}
    made = {}
    for i in range(n):
        for s in range(n.bit_length() - 1):
            if (i >> s) & 1:
                start = (i >> (s + 1)) << (s + 1)
                reads[i, s] = (start, start + (1 << s))
    def make(start, stop):
        if stop - start == 1 or (start, stop) in made:
            return
        mid = (start + stop) // 2
        make(start, mid)
        make(mid, stop)
        made[start, stop] = len(joins)
        joins.append((start, mid, stop))
    for i in range(n):
        for s in range(n.bit_length() - 1):
            if (i, s) in reads:
                make(*reads[i, s])
    return joins, made, reads


def mixer_kernel(
    head_bits, cross, seq_size,
    q_hbm, k_hbm, v_hbm, res_hbm, w_hbm, decay_hbm, codes_hbm, scale_hbm, pos_hbm, gain_hbm, out,
    q, k, v, res, w, decay, codes, scale, pos, gain, hid, fu, sent, came, b_all, reads_all, state, raw, runs, y, ex, ef,
    lam, fac, spread, gone, gone_in, gone_chip, gone_prev, s_bf, s_in, carried, pay,
    small_sem, in_sem, kv_sem, w_sem, halo_send, halo_recv, wx_sem, gone_sem, bc_send, bc_recv, s_send, s_recv,
    z_send, z_far, z_recv, f_send, f_recv, far_sem,
):
    rows_total, width = q.shape
    n = rows_total // CHUNK
    ssm = decay.shape[0]
    inner = n.bit_length() - 1
    low_levels = CHUNK.bit_length()
    first_level = rows_total.bit_length()
    half = width // 2
    head_pos = lax.axis_index("head")
    z = lax.axis_index("seq")
    f = lax.axis_index("fsdp")
    sibling = {"fsdp": 1 - f}
    ahead = {"seq": z + 1}
    after = {"seq": z + f, "fsdp": 1 - f}
    has_next = z + 1 < seq_size
    has_prev = z > 0
    has_after = jnp.logical_or(f == 0, has_next)
    has_before = jnp.logical_or(f == 1, has_prev)

    def head_partner(bit):
        up = lax.rem(head_pos // (1 << bit), 2)
        return {"head": head_pos + (1 << bit) * (1 - 2 * up)}

    def rows_of(c):
        if isinstance(c, int):
            return pl.ds(c * CHUNK, CHUNK)
        return pl.ds(pl.multiple_of(c * CHUNK, CHUNK), CHUNK)

    def next_rows(c):
        if isinstance(c, int):
            return pl.ds((c + 1) * CHUNK, CHUNK)
        return pl.ds(pl.multiple_of((c + 1) * CHUNK, CHUNK), CHUNK)

    def load_k(c):
        return pltpu.make_async_copy(k_hbm.at[rows_of(c)], k.at[next_rows(c)], kv_sem.at[0, c])

    def load_v(c):
        return pltpu.make_async_copy(v_hbm.at[rows_of(c)], v.at[next_rows(c)], kv_sem.at[1, c])

    def load_q(c):
        return pltpu.make_async_copy(q_hbm.at[rows_of(c)], q.at[rows_of(c)], in_sem.at[0, c])

    def load_res(c):
        return pltpu.make_async_copy(res_hbm.at[rows_of(c)], res.at[rows_of(c)], in_sem.at[1, c])

    def remote(src, dst, send, recv, device):
        return pltpu.make_async_remote_copy(src, dst, send, recv, device_id=device, device_id_type=MESH)

    barrier = pltpu.get_barrier_semaphore()

    def greet(device):
        pl.semaphore_signal(barrier, inc=1, device_id=device, device_id_type=MESH)

    for bit in range(head_bits):
        greet(head_partner(bit))
    greet(sibling)

    @pl.when(has_next)
    def _():
        greet(ahead)

    @pl.when(has_prev)
    def _():
        greet({"seq": z - 1})


    @pl.when(jnp.logical_and(f == 1, has_next))
    def _():
        greet(after)

    @pl.when(jnp.logical_and(f == 0, has_prev))
    def _():
        greet({"seq": z - 1, "fsdp": 1 - f})

    smalls = [
        pltpu.make_async_copy(src, dst, small_sem.at[number])
        for number, (src, dst) in enumerate(
            [(decay_hbm, decay), (codes_hbm, codes), (scale_hbm, scale), (pos_hbm, pos), (gain_hbm, gain)]
        )
    ]
    for copy in smalls:
        copy.start()
    depth = w_hbm.shape[0]
    own_rows = pl.ds(pl.multiple_of(f * depth, depth), depth)
    w_load = pltpu.make_async_copy(w_hbm, w.at[own_rows], w_sem)
    w_load.start()
    load_k(0).start()
    load_v(0).start()
    order = [(i + 1) % n for i in range(n)]
    links = head_bits + 1
    links += has_next.astype(jnp.int32) + has_prev.astype(jnp.int32)
    links += jnp.logical_and(f == 1, has_next).astype(jnp.int32) + jnp.logical_and(f == 0, has_prev).astype(jnp.int32)
    pl.semaphore_wait(barrier, links)
    @pl.when(jnp.logical_and(has_prev, has_next))
    def _():
        pl.semaphore_signal(far_sem, inc=1, device_id={"seq": z - 1}, device_id_type=MESH)

    tail = pl.ds(rows_total - WINDOW, WINDOW)
    halo = [
        remote(k_hbm.at[tail], k.at[pl.ds(0, WINDOW)], halo_send.at[0], halo_recv.at[0], after),
        remote(v_hbm.at[tail], v.at[pl.ds(0, WINDOW)], halo_send.at[1], halo_recv.at[1], after),
    ]

    @pl.when(has_after)
    def _():
        for copy in halo:
            copy.start()

    w_send = remote(w_hbm, w.at[own_rows], wx_sem.at[0], wx_sem.at[1], sibling)
    w_send.start()
    for c in order:
        if c:
            load_k(c).start()
            load_v(c).start()
        load_q(c).start()
        load_res(c).start()

    @pl.when(jnp.logical_not(has_before))
    def _():
        k[:CHUNK, :] = jnp.zeros((CHUNK, width), BF16)
        v[:CHUNK, :] = jnp.zeros((CHUNK, width), BF16)

    for copy in smalls:
        copy.wait()

    tri = jnp.where(iota((CHUNK, CHUNK), 1) <= iota((CHUNK, CHUNK), 0), 1.0, 0.0)
    decays = decay[...] * LOG2E
    stacked = jnp.concatenate([decays[:, c * CHUNK : (c + 1) * CHUNK] for c in range(n)], axis=0)
    sums = dot_nt(tri, stacked, lax.Precision.HIGHEST)
    total = sums[CHUNK - 1 :, :]
    rise = split2(jnp.exp2(0.5 * total - sums))
    fall = split2(jnp.exp2(sums - 0.5 * total))
    for c in range(n):
        parts = [side[:, a * n * ssm + c * ssm : a * n * ssm + (c + 1) * ssm] for side in (rise, fall) for a in range(2)]
        ef[c] = jnp.concatenate(parts, axis=1)
    tot = [total[:, c * ssm : (c + 1) * ssm] for c in range(n)]
    joins, made, reads = plan(n)

    def between(start, stop):
        return functools.reduce(lambda a, b: a + b, tot[start:stop], jnp.zeros_like(tot[0]))

    table = []

    def put(exponent):
        table.append(exponent)
        return len(table) - 1

    for c in range(n):
        put(0.5 * tot[c] + between(c + 1, n))
    for c in range(n):
        put(0.5 * tot[c] + between(0, c))
    all_row = put(between(0, n))

    def own_half(start, stop):
        return 0.5 * tot[start] if stop - start == 1 else jnp.zeros_like(tot[0])

    join_rows = [
        (put(own_half(start, mid) + between(mid, stop)), put(own_half(mid, stop))) for start, mid, stop in joins
    ]
    read_rows = {
        (i, s): put(own_half(*reads[i, s]) + between(reads[i, s][1], i) + 0.5 * tot[i]) for (i, s) in sorted(reads)
    }
    while len(table) % 16:
        put(jnp.zeros_like(tot[0]))
    same = lax.rem(iota((2 * ssm, width), 0), ssm) == iota((2 * ssm, width), 1) // HEAD_VALUES
    spread[...] = jnp.where(same, 1.0, 0.0).astype(BF16)
    fac[...] = dot(split2(jnp.exp2(-jnp.concatenate(table, axis=0))), spread[...])
    gone[...] = jnp.broadcast_to(fac[all_row : all_row + 1, :], gone.shape)
    eye = jnp.where(iota((CHUNK, CHUNK), 1) == iota((CHUNK, CHUNK), 0), 1.0, 0.0).astype(BF16)
    for c in range(n):
        code = codes[:, c * CHUNK : (c + 1) * CHUNK].astype(F32).astype(BF16)
        lam[c] = dot_nt(eye, code) * scale[...]

    gone_send = remote(gone, gone_in, gone_sem.at[0], gone_sem.at[1], sibling)
    gone_send.start()

    def bc_copy(kind, bit, c):
        return remote(
            sent.at[kind, bit, rows_of(c)], came.at[kind, bit, rows_of(c)], bc_send.at[kind, bit, c],
            bc_recv.at[kind, bit, c], head_partner(bit),
        )

    def summed(kind, c):
        rows = rows_of(c)
        value = sent[kind, 0, rows, :]
        for bit in range(head_bits):
            bc_copy(kind, bit, c).wait_recv()
            value = (sent[kind, bit, rows, :].astype(F32) + came[kind, bit, rows, :].astype(F32)).astype(BF16)
            if bit < head_bits - 1:
                sent[kind, bit + 1, rows, :] = value
                bc_copy(kind, bit + 1, c).start()
        return value

    def collect(c):
        rows = rows_of(c)
        b = summed(0, c)
        b_all[rows, :] = b
        chunk = dot_tn(b, fu[rows, :])
        raw[c] = chunk
        state[...] += chunk * fac[pl.ds(c, 1), :]

    state[...] = jnp.zeros_like(state)

    load_k(0).wait()
    load_v(0).wait()
    w_load.wait()
    w_send.wait()
    near = (iota((CHUNK, CHUNK), 0) - iota((CHUNK, CHUNK), 1)).astype(F32)
    far = near + float(WINDOW)
    factor = LOG2E / math.sqrt(HEAD_DIM)

    def attend(i, carry):
        c = lax.rem(i + 1, n)

        @pl.when(i < n - 1)
        def _():
            load_k(c).wait()
            load_v(c).wait()

        @pl.when(jnp.logical_and(i == n - 1, has_before))
        def _():
            for copy in halo:
                copy.wait_recv()

        load_q(c).wait()
        load_res(c).wait()
        rows = rows_of(c)
        both = pl.ds(pl.multiple_of(c * CHUNK, CHUNK), 2 * CHUNK)
        pos_col = jnp.broadcast_to(pos[c].astype(F32), (CHUNK, CHUNK)).T
        mask_cur = jnp.where((near >= 0) & (near <= pos_col), 0.0, -jnp.inf)
        mask_prev = jnp.where((far < float(WINDOW)) & (far <= pos_col), 0.0, -jnp.inf)
        mask = jnp.concatenate([mask_prev, mask_cur], axis=1)
        heads = [slice(h * HEAD_DIM, (h + 1) * HEAD_DIM) for h in range(width // HEAD_DIM)]
        scores = [dot_nt(q[rows, cols], k[both, cols]) + mask for cols in heads]
        tops = [jnp.max(s, axis=1, keepdims=True) for s in scores]
        raised = [jnp.exp2((s - top) * factor) for s, top in zip(scores, tops)]
        ones = jnp.ones((2 * CHUNK, HEAD_DIM), BF16)
        mixed = [dot(e.astype(BF16), jnp.concatenate([v[both, cols], ones], axis=1)) for e, cols in zip(raised, heads)]
        weighted = [m[:, :HEAD_DIM] for m in mixed]
        totals = [m[:, HEAD_DIM:] for m in mixed]
        hidden = jnp.concatenate(
            [
                (res[rows, cols].astype(F32) + a * (1.0 / t)).astype(BF16)
                for cols, a, t in zip(heads, weighted, totals)
            ],
            axis=1,
        )
        hid[rows, :] = hidden

        part = dot(hidden, w[...]).astype(BF16)
        sent[0, 0, rows, :] = part[:, :STATES]
        sent[1, 0, rows, :] = part[:, STATES:]
        if head_bits:
            bc_copy(0, 0, c).start()
        fu[rows, :] = (dot(ef[c][:, 2 * ssm :], spread[...]) * hidden.astype(F32)).astype(BF16)
        return carry

    lax.fori_loop(0, n, attend, 0)
    gone_send.wait()
    first_core = f == 0
    mine = gone[0:1, :]
    theirs = gone_in[0:1, :]
    gone_chip[...] = jnp.broadcast_to(mine * theirs, gone_chip.shape)
    gone_in[1:2, :] = jnp.where(first_core, theirs, mine)
    gone_in[2:3, :] = mine * theirs
    gone_in[3:4, :] = jnp.where(first_core, 1.0, theirs)
    chip_send = remote(gone_chip, gone_prev, gone_sem.at[2], gone_sem.at[3], ahead)

    @pl.when(has_next)
    def _():
        chip_send.start()

    if head_bits:
        for number in range(n):
            bc_copy(1, 0, order[number]).start()
    for number in range(n):
        collect(order[number])

    pieces = half // PIECE if half % PIECE == 0 else 1
    step = half // pieces

    def own_piece(p):
        return pl.ds(pl.multiple_of(f * half + p * step, step), step)

    def other_piece(p):
        return pl.ds(pl.multiple_of((1 - f) * half + p * step, step), step)

    def s_copy(p):
        cols = other_piece(p)
        return remote(s_bf.at[:, cols], s_in.at[:, cols], s_send.at[p], s_recv.at[p], sibling)

    own_cols = pl.ds(pl.multiple_of(f * half, half), half)
    rest = remote(s_bf.at[:, own_cols], s_in.at[:, own_cols], s_send.at[pieces], s_recv.at[pieces], sibling)
    for p in range(pieces):
        s_bf[:, other_piece(p)] = state[:, other_piece(p)].astype(BF16)
        s_copy(p).start()
    s_bf[:, own_cols] = state[:, own_cols].astype(BF16)

    @pl.when(first_core)
    def _():
        rest.start()

    side = (CHUNK, CHUNK)
    differ = iota(side, 0) ^ iota(side, 1)
    causal = iota(side, 1) <= iota(side, 0)

    def run_of(start, stop):
        return raw[start] if stop - start == 1 else runs[made[start, stop]]

    def local(i):
        rows = rows_of(i)
        lam_c = lam[i]
        weight = jnp.broadcast_to(lam_c[:, 0:1], side)
        for level in range(1, low_levels):
            weight = jnp.where(differ >= 1 << level - 1, lam_c[:, level : level + 1], weight)
        b, c = b_all[rows, :], summed(1, i)
        shared = jnp.where(causal, dot_nt(c, b) * weight, 0.0)
        left = [shared.astype(BF16)]
        right = [fu[rows, :]]
        c32 = c.astype(F32)
        for s in range(inner):
            if (i, s) in reads:
                row = read_rows[i, s]
                left.append((c32 * lam_c[:, low_levels + s : low_levels + s + 1]).astype(BF16))
                right.append((run_of(*reads[i, s]) * fac[row : row + 1, :]).astype(BF16))
        for s in range(cross):
            reads_all[rows, s * STATES : (s + 1) * STATES] = (
                c32 * lam_c[:, first_level + s : first_level + s + 1]
            ).astype(BF16)
        terms = dot(jnp.concatenate(left, axis=1), jnp.concatenate(right, axis=0))
        grow = dot(ef[i][:, : 2 * ssm], spread[...])
        y[rows, :] = terms * grow
        ex[rows, :] = grow * fac[n + i : n + i + 1, :]

    def z_copy(level, p):
        return remote(
            pay.at[level, :, pl.ds(p * step, step)], carried.at[level, :, own_piece(p)], z_send.at[level, p],
            z_recv.at[level, p], ahead,
        )

    def far_copy(level, p):
        return remote(
            pay.at[level, :, pl.ds(p * step, step)], carried.at[level, :, own_piece(p)], z_far.at[level, p],
            z_recv.at[level, p], {"seq": z + 2},
        )

    def forward(level, p):
        cols = own_piece(p)
        return remote(
            carried.at[level, :, cols], carried.at[level, :, cols], f_send.at[level, p], f_recv.at[level, p], sibling
        )

    def bit_of(x, level):
        return lax.rem(x // (1 << level - 1), 2) == 1

    def takes(level):
        return bit_of(z, level)

    def gives(level):
        return jnp.logical_and(has_next, bit_of(z + 1, level))

    def direct(level, p):
        return level > 1 and p >= (pieces + 1) // 2

    def place(level):
        return lax.rem(z, 1 << level - 1)

    def sends_near(level, p):
        if direct(level, p):
            return jnp.logical_and(gives(level), jnp.logical_or(jnp.logical_not(takes(level)), place(level) > 0))
        return gives(level)

    def sends_far(level):
        return jnp.logical_and(gives(level), jnp.logical_not(takes(level)))

    def give_run(level, p):
        if level < cross:

            @pl.when(sends_far(level))
            def _():
                pay[level, :, p * step : (p + 1) * step] = state[:, own_piece(p)].astype(BF16)
                if direct(level, p):
                    far_copy(level, p).start()
                z_copy(level, p).start()

    def handle(level, p):
        @pl.when(takes(level))
        def _():
            cols = own_piece(p)
            z_copy(level, p).wait_recv()
            if direct(level, p):

                @pl.when(place(level) == 1)
                def _():
                    carried[level, :, cols] = (carried[level, :, cols].astype(F32) * gone_prev[0:1, cols]).astype(BF16)

            forward(level, p).start()
            moved = carried[level, :, cols].astype(F32) * gone_in[2:3, cols]

            @pl.when(sends_near(level, p))
            def _():
                pay[level, :, p * step : (p + 1) * step] = moved.astype(BF16)
                z_copy(level, p).start()

            state[:, cols] += moved
            give_run(level + 1, p)

    @pl.when(has_prev)
    def _():
        chip_send.wait_recv()

    @pl.when(z + 2 < seq_size)
    def _():
        pl.semaphore_wait(far_sem, 1)

    for p in range(pieces):
        cols = own_piece(p)
        s_copy(p).wait_recv()
        mine_s = state[:, cols]
        theirs_s = s_in[:, cols].astype(F32)
        state[:, cols] = jnp.where(first_core, mine_s, theirs_s) * gone_in[1:2, cols] + jnp.where(
            first_core, theirs_s, mine_s
        )
        give_run(1, p)
    for level in range(1, cross):

        @pl.when(jnp.logical_not(takes(level)))
        def _():
            carried[level] = jnp.zeros((STATES, width), BF16)

    for number, (start, mid, stop) in enumerate(joins):
        one, two = join_rows[number]
        runs[number] = run_of(start, mid) * fac[one : one + 1, :] + run_of(mid, stop) * fac[two : two + 1, :]
    for number in range(n // 4):
        local(order[number])
    for level in range(1, cross - 1):
        for p in range(pieces):
            handle(level, p)
    for number in range(n // 4, n):
        local(order[number])

    @pl.when(first_core)
    def _():
        carried[0] = jnp.zeros((STATES, width), BF16)

    @pl.when(jnp.logical_not(first_core))
    def _():
        rest.wait_recv()
        carried[0] = s_in[...]

    per_unit = UNIT // step if half % UNIT == 0 else 1
    unit = per_unit * step
    side = (unit, unit)
    group = jnp.where(
        iota(side, 0) // HEAD_VALUES == iota(side, 1) // HEAD_VALUES, 1.0 / HEAD_VALUES, 0.0
    ).astype(BF16)
    last = cross - 1

    def finish(cols):
        shift = gone_in[3:4, cols]
        held = [carried[0, :, cols]]
        held += [(carried[level, :, cols].astype(F32) * shift).astype(BF16) for level in range(1, cross)]
        held = jnp.concatenate(held, axis=0)
        bands = [slice(r * 2 * CHUNK, (r + 1) * 2 * CHUNK) for r in range(rows_total // (2 * CHUNK))]
        terms = [y[rows, cols] + dot(reads_all[rows, :], held) * ex[rows, cols] for rows in bands]
        means = [dot((term * term).astype(BF16), group) for term in terms]
        for rows, term, mean in zip(bands, terms, means):
            out[rows, cols] = (
                hid[rows, cols].astype(F32) + term * lax.rsqrt(mean + 1e-05) * gain[:, cols]
            ).astype(BF16)

    units = half // unit
    turned = jnp.logical_and(takes(last), place(last) > 0)

    @pl.when(gives(last))
    def _():
        for p in range(pieces):
            if not direct(last, p):
                handle(last, p)

    def handle_unit(number):
        for p in range(number * per_unit, (number + 1) * per_unit):
            if direct(last, p):
                handle(last, p)
            else:

                @pl.when(jnp.logical_not(gives(last)))
                def _():
                    handle(last, p)

    def wait_unit(number):
        for level in range(1, cross):

            @pl.when(takes(level))
            def _():
                for p in range(number * per_unit, (number + 1) * per_unit):
                    forward(level, p).wait_recv()

    def in_turn(turn, act):
        if units == 1:
            act(turn)
            return

        @pl.when(jnp.logical_not(turned))
        def _():
            act(turn)

        @pl.when(turned)
        def _():
            act(units - 1 - turn)

    for turn in range(units):
        in_turn(turn, handle_unit)
        number = jnp.where(turned, units - 1 - turn, turn)
        finish(pl.ds(pl.multiple_of(f * half + number * unit, unit), unit))
        in_turn(turn, wait_unit)
        finish(pl.ds(pl.multiple_of((1 - f) * half + number * unit, unit), unit))

    @pl.when(has_after)
    def _():
        for copy in halo:
            copy.wait_send()

    for bit in range(head_bits):
        for c in range(n):
            for kind in range(2):
                bc_copy(kind, bit, c).wait_send()
    for p in range(pieces):
        s_copy(p).wait_send()
        for level in range(1, cross):

            @pl.when(takes(level))
            def _():
                forward(level, p).wait_send()

            @pl.when(sends_near(level, p))
            def _():
                z_copy(level, p).wait_send()

            if direct(level, p):

                @pl.when(sends_far(level))
                def _():
                    far_copy(level, p).wait_send()

    @pl.when(has_next)
    def _():
        chip_send.wait_send()

    @pl.when(first_core)
    def _():
        rest.wait_send()


def body(
    residual_in,
    query_rows,
    key_rows,
    value_rows,
    bc_weight,
    decay_rate,
    level_codes,
    level_scale,
    positions,
    ssm_gain,
):
    rows, width = residual_in.shape
    n = rows // CHUNK
    ssm = decay_rate.shape[1]
    seq_size = lax.axis_size("seq")
    head_bits = lax.axis_size("head").bit_length() - 1
    cross = (seq_size * lax.axis_size("fsdp")).bit_length() - 1
    bits = max(head_bits, 1)
    joins, _, reads = plan(n)
    factors = 2 * n + 1 + 2 * len(joins) + len(reads)
    factors += -factors % 16
    half = width // 2
    pieces = half // PIECE if half % PIECE == 0 else 1
    levels = level_codes.shape[1]
    dma = pltpu.SemaphoreType.DMA
    any_spec = pl.BlockSpec(memory_space=pl.ANY)
    scratch = [
        pltpu.VMEM((rows, width), BF16),
        pltpu.VMEM((rows + CHUNK, width), BF16),
        pltpu.VMEM((rows + CHUNK, width), BF16),
        pltpu.VMEM((rows, width), BF16),
        pltpu.VMEM((2 * bc_weight.shape[0], bc_weight.shape[1]), BF16),
        pltpu.VMEM((ssm, rows), F32),
        pltpu.VMEM((levels, rows), jnp.int32),
        pltpu.VMEM((1, levels), F32),
        pltpu.VMEM((n, 1, CHUNK), jnp.int32),
        pltpu.VMEM((1, width), F32),
        pltpu.VMEM((rows, width), BF16),
        pltpu.VMEM((rows, width), BF16),
        pltpu.VMEM((2, bits, rows, STATES), BF16),
        pltpu.VMEM((2, bits, rows, STATES), BF16),
        pltpu.VMEM((rows, STATES), BF16),
        pltpu.VMEM((rows, cross * STATES), BF16),
        pltpu.VMEM((STATES, width), F32),
        pltpu.VMEM((n, STATES, width), F32),
        pltpu.VMEM((len(joins), STATES, width), F32),
        pltpu.VMEM((rows, width), F32),
        pltpu.VMEM((rows, width), F32),
        pltpu.VMEM((n, CHUNK, 4 * ssm), BF16),
        pltpu.VMEM((n, CHUNK, level_codes.shape[1]), F32),
        pltpu.VMEM((factors, width), F32),
        pltpu.VMEM((2 * ssm, width), BF16),
        pltpu.VMEM((8, width), F32),
        pltpu.VMEM((8, width), F32),
        pltpu.VMEM((8, width), F32),
        pltpu.VMEM((8, width), F32),
        pltpu.VMEM((STATES, width), BF16),
        pltpu.VMEM((STATES, width), BF16),
        pltpu.VMEM((cross, STATES, width), BF16),
        pltpu.VMEM((cross, STATES, width // 2), BF16),
        dma((5,)), dma((2, n)), dma((2, n)), dma, dma((2,)), dma((2,)), dma((2,)), dma((4,)),
        dma((2, bits, n)), dma((2, bits, n)), dma((pieces + 1,)), dma((pieces + 1,)),
        dma((cross, pieces)), dma((cross, pieces)), dma((cross, pieces)), dma((cross, pieces)), dma((cross, pieces)),
        pltpu.SemaphoreType.REGULAR,
    ]
    return pl.pallas_call(
        functools.partial(mixer_kernel, head_bits, cross, seq_size),
        in_specs=[any_spec] * 10,
        out_specs=pl.BlockSpec(memory_space=pltpu.VMEM),
        out_shape=pltpu.VMEM((rows, width), BF16),
        scratch_shapes=scratch,
        name="attend_and_mix",
        compiler_params=pltpu.CompilerParams(collective_id=0, has_side_effects=True, vmem_limit_bytes=56 * 2**20),
        cost_estimate=pl.CostEstimate(flops=rows * width * 8000, bytes_accessed=12 * rows * width, transcendentals=0),
    )(
        query_rows, key_rows, value_rows, residual_in, bc_weight, decay_rate.T, level_codes.T, level_scale[None, :],
        positions.reshape(n, 1, CHUNK), ssm_gain[None, :],
    )


def solution(mesh):
    in_specs = (
        P(("groups", "seq", "fsdp"), "head"),
        P(("groups", "seq", "fsdp"), "head"),
        P(("groups", "seq", "fsdp"), "head"),
        P(("groups", "seq", "fsdp"), "head"),
        P(("head", "fsdp"), None),
        P(("groups", "seq", "fsdp"), "head"),
        P(("groups", "seq", "fsdp"), None),
        P(),
        P(("groups", "seq", "fsdp")),
        P("head"),
    )
    out_specs = P(("groups", "seq", "fsdp"), "head")
    return jax.shard_map(body, mesh=mesh, in_specs=in_specs, out_specs=out_specs, check_vma=False)
```
